512 devices in a mesh: ply: 8 (over y_lo, x), stripe: 64 (over z, y_hi, core).
Axes of the slice: x: 4, y: 8 (y_hi: 4, y_lo: 2; y = y_hi * 2 + y_lo), z: 8, core: 2. Of those that a mesh axis runs over, the one named last changes fastest.
Arguments:
- displacement: float32 [3, 8, 4, 512, 512], P(None, 'ply', None, 'stripe'), may hold values from -5 to 5
- velocity: float32 [3, 8, 4, 512, 512], P(None, 'ply', None, 'stripe'), may hold values from -5 to 5
- acceleration: float32 [3, 8, 4, 512, 512], P(None, 'ply', None, 'stripe'), may hold values from -5 to 5
- fibre_codes: int32 [8, 2], P('ply'), may hold values from 0 to 3
- contact_mask: int32 [512, 512], P('stripe'), may hold values 0 or 1
- bond_flags: int32 [8, 2, 64, 64], P('ply', None, 'stripe'), may hold values from 0 to 1073741823, as said below
Outputs:
- new_displacement: float32 [3, 8, 4, 512, 512], P(None, 'ply', None, 'stripe')
- new_velocity: float32 [3, 8, 4, 512, 512], P(None, 'ply', None, 'stripe')
- new_acceleration: float32 [3, 8, 4, 512, 512], P(None, 'ply', None, 'stripe')
The draws below stay inside these ranges and needn't reach their ends.
Inputs may be any that keep to these rules, and one draw needn't show every extreme that they name: `fibre_codes`: codes 0, 1, 2 and 3 stand for fibres at 0, 90, 45 and -45 degrees in the pair's frame. `contact_mask`: a point in contact with the impactor is 1. `bond_flags`: word 0 holds classes 0 to 29 in bits 0 to 29, word 1 classes 30 to 46 in bits 0 to 16; higher bits are zero; in every draw one block of the lowest pair has all its bonds to the pair above broken.
All inputs are finite; a program needn't handle non-finite values. No bound on the sum of `contact_mask` on one device may be relied on, other than what follows from the above.
Results may differ from the reference program's by a relative error of at most 0.0003.
Values sent between devices are 32-bit elements; how exact they have to be, the bound alone decides.
No kernel may reach another device: no remote copies, remote signals or barrier semaphores. Data moves between devices by JAX's collectives and lax.ppermute only.
A program may use at most 64 MiB of HBM per device.

```python
import jax
import jax.numpy as jnp
from jax import lax

W = 8
LAYERS = 4
PAIRS = 8
NXY = 512
BLOCKS = 64


def draw_bond_flags(key, part):
    key_first, key_second, key_row, key_col = jax.random.split(key, 4)
    flag_shape = (PAIRS, 2, BLOCKS, BLOCKS)
    first_bits = jax.random.randint(key_first, flag_shape, 0, 2 ** 30, dtype=jnp.int32)
    second_bits = jax.random.randint(key_second, flag_shape, 0, 2 ** 30, dtype=jnp.int32)
    limits = jnp.array([2 ** 30 - 1, 2 ** 17 - 1], dtype=jnp.int32)[None, :, None, None]
    flag_words = first_bits & second_bits & limits
    row_pick = jax.random.randint(key_row, (), 0, BLOCKS, dtype=jnp.int32)
    col_pick = jax.random.randint(key_col, (), 0, BLOCKS, dtype=jnp.int32)
    pair_ids = jnp.arange(PAIRS, dtype=jnp.int32)[:, None, None, None]
    row_ids = jnp.arange(BLOCKS, dtype=jnp.int32)[None, None, :, None]
    col_ids = jnp.arange(BLOCKS, dtype=jnp.int32)[None, None, None, :]
    chosen = (pair_ids == 0) & (row_ids == row_pick) & (col_ids == col_pick)
    return jnp.where(chosen, limits, flag_words).astype(jnp.int32)


def touch_ends(result, own_key, smallest, top_value):
    spot = [jax.random.randint(jax.random.fold_in(own_key, axis), (), 0, length) for axis, length in enumerate(result.shape)]
    main_axis = result.shape.index(max(result.shape))
    next_to = spot[:main_axis] + [(spot[main_axis] + 1) % result.shape[main_axis]] + spot[main_axis + 1:]
    return result.at[tuple(spot)].set(smallest).at[tuple(next_to)].set(top_value)


def level_of(own_key, dims, cuts, smallest, high):
    level, own = 1.0, jax.random.fold_in(own_key, 6)
    for position, blocks in cuts:
        steps = jnp.exp(jax.random.uniform(jax.random.fold_in(own, position), (blocks,), jnp.float32, smallest / len(cuts), high / len(cuts)))
        level = level * jnp.repeat(steps, dims[position] // blocks).reshape([-1 if axis == position else 1 for axis in range(len(dims))])
    return level


def scatter_about(rng, shape, width, limit, cuts=(), held_as=jnp.bfloat16):
    drawn = width * jax.random.normal(rng, shape, jnp.float32)
    if cuts:
        drawn = drawn * level_of(rng, shape, cuts, -0.22, 0.18)
    return jnp.clip(drawn, -limit, limit).astype(held_as)


def setup_inputs(seed: int = 0) -> dict:
    streams_of = jax.random.split(jax.random.key(seed), 7)
    displacement = scatter_about(streams_of[0], (3, PAIRS, LAYERS, NXY, NXY), 1.0, 5.0, ((1, 8), (3, 64)), jnp.float32)
    velocity = scatter_about(streams_of[1], (3, PAIRS, LAYERS, NXY, NXY), 1.0, 5.0, ((1, 8), (3, 64)), jnp.float32)
    acceleration = scatter_about(streams_of[2], (3, PAIRS, LAYERS, NXY, NXY), 1.0, 5.0, ((1, 8), (3, 64)), jnp.float32)
    fibre_codes = touch_ends(jax.random.randint(streams_of[3], (PAIRS, 2), 0, 4), jax.random.fold_in(streams_of[3], 1), 0, 3).astype(jnp.int32)
    contact_mask = touch_ends((jax.random.randint(streams_of[4], (NXY, NXY), 0, 4) < 1).astype(jnp.int32), jax.random.fold_in(streams_of[4], 1), 0, 1)
    bond_flags = draw_bond_flags(jax.random.fold_in(streams_of[6], 71), 0)
    return dict(displacement=displacement, velocity=velocity, acceleration=acceleration, fibre_codes=fibre_codes, contact_mask=contact_mask, bond_flags=bond_flags)


ROOT_HALF = 0.7071067811865476
RATE = 0.025
MATRIX_C = 1.0
FIBRE_C = 4.0
INTER_C = 1.5
IMPACT = 2.0


def bond_offsets():
    offsets_found = []
    for along_z in range(-3, 4):
        for along_i in range(-3, 4):
            for along_j in range(-3, 4):
                radius = along_z * along_z + along_i * along_i + along_j * along_j
                if 0 < radius <= 9:
                    offsets_found.append((along_z, along_i, along_j))
    return offsets_found


def interface_offsets():
    offsets_found = []
    for along_z in range(1, 4):
        for along_i in range(-3, 4):
            for along_j in range(-3, 4):
                radius = along_z * along_z + along_i * along_i + along_j * along_j
                if radius <= 9:
                    offsets_found.append((along_z, along_i, along_j))
    return offsets_found


def fibre_table(code_pair):
    levels = jnp.arange(4, dtype=jnp.int32)
    matches = (code_pair[:, None] == levels[None, :]).astype(jnp.float32)
    cos_parts = jnp.sum(matches * jnp.array([1.0, 0.0, ROOT_HALF, ROOT_HALF], jnp.float32), axis=1)
    sin_parts = jnp.sum(matches * jnp.array([0.0, 1.0, ROOT_HALF, -ROOT_HALF], jnp.float32), axis=1)
    return cos_parts, sin_parts


def layer_coeffs(cos_parts, sin_parts, offset):
    along_z, along_i, along_j = offset
    radius = float(along_z * along_z + along_i * along_i + along_j * along_j)
    entries = []
    for layer_index in range(4):
        other_layer = min(max(layer_index + along_z, 0), 3)
        weight_here = (along_i * cos_parts[layer_index // 2] + along_j * sin_parts[layer_index // 2]) ** 2 / radius
        weight_there = (along_i * cos_parts[other_layer // 2] + along_j * sin_parts[other_layer // 2]) ** 2 / radius
        entries.append(MATRIX_C + FIBRE_C * 0.5 * (weight_here + weight_there))
    return jnp.stack(entries) * (RATE / radius ** 1.5)


def pair_terms(padded, inside, advanced, cos_parts, sin_parts):
    row_count = advanced.shape[2]
    plate_cells = advanced.shape[3]
    force_i = jnp.zeros(advanced.shape[1:], jnp.float32)
    force_j = jnp.zeros(advanced.shape[1:], jnp.float32)
    force_z = jnp.zeros(advanced.shape[1:], jnp.float32)
    for offset in bond_offsets():
        along_z, along_i, along_j = offset
        coeffs = layer_coeffs(cos_parts, sin_parts, offset)
        facing = padded[:, 3 + along_z:7 + along_z, 3 + along_i:3 + along_i + row_count, 3 + along_j:3 + along_j + plate_cells]
        present = inside[3 + along_z:7 + along_z, 3 + along_i:3 + along_i + row_count, 3 + along_j:3 + along_j + plate_cells]
        stretch = along_i * (facing[0] - advanced[0]) + along_j * (facing[1] - advanced[1]) + along_z * (facing[2] - advanced[2])
        bond_term = coeffs[:, None, None] * present * stretch
        force_i = force_i + along_i * bond_term
        force_j = force_j + along_j * bond_term
        force_z = force_z + along_z * bond_term
    return jnp.stack([force_i, force_j, force_z])


def interface_terms(lower_layers, facing_pad, plane_ok, flag_cells, has_upper):
    row_count = lower_layers.shape[2]
    plate_cells = lower_layers.shape[3]
    lower_force = [jnp.zeros((3, row_count, plate_cells), jnp.float32)] * 4
    reaction = [jnp.zeros((3, row_count + 6, plate_cells + 6), jnp.float32)] * 3
    for class_index, offset in enumerate(interface_offsets()):
        along_z, along_i, along_j = offset
        radius = float(along_z * along_z + along_i * along_i + along_j * along_j)
        bit_values = jnp.right_shift(flag_cells[class_index // 30], class_index % 30) & 1
        intact = (1 - bit_values).astype(jnp.float32) * has_upper
        bond_scale = intact * plane_ok[3 + along_i:3 + along_i + row_count, 3 + along_j:3 + along_j + plate_cells] * (INTER_C * RATE / radius ** 1.5)
        for layer_index in range(4 - along_z, 4):
            upper_index = layer_index + along_z - 4
            facing = facing_pad[:, upper_index, 3 + along_i:3 + along_i + row_count, 3 + along_j:3 + along_j + plate_cells]
            own_disp = lower_layers[:, layer_index]
            stretch = along_i * (facing[0] - own_disp[0]) + along_j * (facing[1] - own_disp[1]) + along_z * (facing[2] - own_disp[2])
            bond_term = bond_scale * stretch
            bond_push = jnp.stack([along_i * bond_term, along_j * bond_term, along_z * bond_term])
            lower_force[layer_index] = lower_force[layer_index] + bond_push
            reaction[upper_index] = reaction[upper_index] + jnp.pad(-bond_push, ((0, 0), (3 + along_i, 3 - along_i), (3 + along_j, 3 - along_j)))
    return jnp.stack(lower_force, axis=1), jnp.stack(reaction, axis=1)[:, :, :, 3:3 + plate_cells]


def pair_force(pieces):
    advanced, code_pair = pieces
    plate_cells = advanced.shape[-1]
    cos_parts, sin_parts = fibre_table(code_pair)
    padded = jnp.pad(advanced, ((0, 0), (3, 3), (3, 3), (3, 3)))
    inside = jnp.pad(jnp.ones((4, plate_cells, plate_cells), jnp.float32), 3)
    return pair_terms(padded, inside, advanced, cos_parts, sin_parts)


def interface_pair(pieces):
    lower_layers, upper_layers, flag_words = pieces
    plate_cells = lower_layers.shape[-1]
    upper_view = jnp.swapaxes(jnp.stack([upper_layers[1], upper_layers[0], upper_layers[2]])[:, 0:3], 2, 3)
    facing_pad = jnp.pad(upper_view, ((0, 0), (0, 0), (3, 3), (3, 3)))
    plane_ok = jnp.pad(jnp.ones((plate_cells, plate_cells), jnp.float32), 3)
    flag_cells = jnp.repeat(jnp.repeat(flag_words, W, axis=1), W, axis=2)
    lower_force, reaction = interface_terms(lower_layers, facing_pad, plane_ok, flag_cells, 1.0)
    reaction = reaction[:, :, 3:3 + plate_cells]
    returned = jnp.swapaxes(jnp.stack([reaction[1], reaction[0], reaction[2]]), 2, 3)
    return lower_force, returned


def reference(displacement, velocity, acceleration, fibre_codes, contact_mask, bond_flags):
    half_velocity = velocity + 0.5 * acceleration
    advanced = displacement + half_velocity
    advanced_pairs = jnp.moveaxis(advanced, 1, 0)
    accel_pairs = lax.map(pair_force, (advanced_pairs, fibre_codes))
    lower_force, returned = lax.map(interface_pair, (advanced_pairs[:-1], advanced_pairs[1:], bond_flags[:-1]))
    accel_pairs = accel_pairs.at[:-1].add(lower_force)
    accel_pairs = accel_pairs.at[1:, :, 0:3].add(returned)
    accel_pairs = accel_pairs.at[-1, 2, 3].add(-IMPACT * contact_mask.astype(jnp.float32))
    fresh_accel = jnp.moveaxis(accel_pairs, 0, 1)
    new_velocity = half_velocity + 0.5 * fresh_accel
    return advanced, new_velocity, fresh_accel
```

```python
import jax
import jax.numpy as jnp
from jax import lax
from jax.experimental import pallas as pl
from jax.experimental.pallas import tpu as pltpu
from jax.sharding import PartitionSpec as P

ROOT_HALF = 0.7071067811865476
RATE = 0.025
MATRIX_C = 1.0
FIBRE_C = 4.0
INTER_C = 1.5
IMPACT = 2.0

F32 = jnp.float32
I32 = jnp.int32
ROWS = 8
TURNS = 64
CELLS = ROWS * TURNS
WINDOW = 12
PLANE = [(di, dj) for di in range(-2, 3) for dj in range(-2, 3)]
INTERPRET = False


def place():
    return lax.axis_index("ply"), lax.axis_index("stripe")


def class_index(dz, di, dj):
    count = 0
    for z in range(1, 4):
        for i in range(-3, 4):
            for j in range(-3, 4):
                if z * z + i * i + j * j <= 9:
                    if (z, i, j) == (dz, di, dj):
                        return count
                    count += 1
    raise ValueError("no class")


def kernel_call(body, outs, scratch, flops):
    return pl.pallas_call(
        body,
        out_shape=outs,
        scratch_shapes=scratch,
        interpret=INTERPRET,
        cost_estimate=pl.CostEstimate(flops=flops, bytes_accessed=2_000_000, transcendentals=0),
        compiler_params=pltpu.CompilerParams(vmem_limit_bytes=32 * 1024 * 1024),
    )


def scaled(factor, value):
    if factor == 1:
        return value
    if factor == -1:
        return -value
    return factor * value


def along(di, dj, first, second):
    if di == 0 and dj == 0:
        return None
    if di == 0:
        return scaled(dj, second)
    if dj == 0:
        return scaled(di, first)
    if abs(di) == abs(dj):
        inner = first + second if di == dj else first - second
        return scaled(di, inner)
    return scaled(di, first) + scaled(dj, second)


def gap(far, near, rise, far_z, near_z):
    total = None if far is None else far - near
    if rise:
        lift = scaled(rise, far_z - near_z)
        total = lift if total is None else total + lift
    return total


def added(total, value):
    return value if total is None else total + value


def lanes_and_cells():
    cell = lax.broadcasted_iota(I32, (8, 128), 0)
    lane = lax.broadcasted_iota(I32, (8, 128), 1)
    return cell, lane


def shifted_by(value, cell):
    after = pltpu.roll(value, 127, 1)
    before = pltpu.roll(value, 1, 1)
    moved = {}
    for dj in (1, 2):
        moved[dj] = pltpu.roll(jnp.where(cell < dj, after, value), 8 - dj, 0)
        moved[-dj] = pltpu.roll(jnp.where(cell >= 8 - dj, before, value), dj, 0)
    return moved, after, before


def advance_kernel(disp, vel, acc, flags, adv, half, down, up, low, high):
    values = []
    for layer in range(4):
        for comp in range(3):
            speed = vel[comp, 0, layer] + 0.5 * acc[comp, 0, layer]
            moved = disp[comp, 0, layer] + speed
            half[comp, 0, layer] = speed
            adv[comp, 0, layer] = moved
            field = 3 * layer + comp
            low[field] = moved[5:8]
            high[field] = moved[0:3]
            values.append(moved)
    for slot, field in enumerate((1, 0, 2, 4, 3, 5, 8)):
        down[8 * slot : 8 * slot + 8] = values[field]
    for slot, field in enumerate((10, 9, 11, 7, 6, 8, 5)):
        up[8 * slot : 8 * slot + 8] = values[field]
    first = flags[0, 0]
    second = flags[0, 1]
    parts = jnp.concatenate(
        [jnp.bitwise_and(first, 0x7FFF), jnp.right_shift(first, 15), second, jnp.zeros((5, TURNS), I32)],
        axis=0,
    ).astype(F32)
    block = lax.broadcasted_iota(I32, (TURNS, CELLS), 0)
    column = lax.broadcasted_iota(I32, (TURNS, CELLS), 1)
    spread = (jnp.right_shift(column, 3) == block).astype(F32)
    up[56:64] = jnp.dot(parts, spread, precision=lax.Precision.HIGHEST, preferred_element_type=F32)


def turn_kernel(above, below, message, turned):
    stacked = jnp.concatenate([above[...], below[...], jnp.zeros((8, CELLS), F32)], axis=0)
    turned[0:8] = jnp.zeros((8, 128), F32)
    turned[CELLS + 8 : CELLS + 16] = jnp.zeros((8, 128), F32)
    for piece in range(4):
        turned[8 + 128 * piece : 136 + 128 * piece] = stacked[:, 128 * piece : 128 * piece + 128].T
    for row in range(WINDOW):
        message[pl.ds(row, TURNS, stride=WINDOW), :] = turned[pl.ds(6 + row, TURNS, stride=8), :]


def coefficient(here, there, dz, di, dj):
    radius = float(dz * dz + di * di + dj * dj)
    level = RATE / radius**1.5
    return level * MATRIX_C + (level * FIBRE_C * 0.5 / radius) * (here + there)


def pair_kernel(adv, low, high, codes, flags, force, own, words, natural, turned, held, moved, far, rates, present, spare):
    ply, stripe = place()
    cell, lane = lanes_and_cells()
    for field in range(12):
        comp, layer = field % 3, field // 3
        whole = adv[comp, 0, layer]
        natural[0, 10 * field : 10 * field + 3] = low[field]
        natural[0, 10 * field + 3 : 10 * field + 10] = whole[0:7]
        natural[1, 10 * field : 10 * field + 7] = whole[1:8]
        natural[1, 10 * field + 7 : 10 * field + 10] = high[field]
    for side in range(2):
        natural[side, 120:128] = jnp.zeros((8, CELLS), F32)
        for piece in range(4):
            turned[side, 128 * piece : 128 * piece + 128] = natural[side, :, 128 * piece : 128 * piece + 128].T
    for position in range(8):
        pick = pl.ds(position, TURNS, stride=8)
        both = jnp.concatenate([turned[0, pick, :], turned[1, pick, :]], axis=0)
        held[128 * position : 128 * position + 128] = both.T
    for field in range(12):
        for q in range(-3, 7):
            value = held[pl.ds(10 * field + q + 3, 8, stride=128), :]
            moved[2, field, q + 3] = value
            if 0 <= q < 4:
                own[field, q] = value
            if -2 <= q < 6:
                others, after, before = shifted_by(value, cell)
                for dj, other in others.items():
                    moved[dj + 2, field, q + 3] = other
                if field % 3 == 1 and 0 <= q < 4:
                    far[0, field // 3, q] = pltpu.roll(jnp.where(cell >= 5, before, value), 3, 0)
                    far[1, field // 3, q] = pltpu.roll(jnp.where(cell < 3, after, value), 5, 0)
    row = 8 * stripe + jnp.where(lane >= TURNS, 4, 0)
    column = 8 * jnp.bitwise_and(lane, TURNS - 1) + cell
    row_in = [(row + q >= 0) & (row + q < CELLS) for q in range(-3, 7)]
    for dj in range(-3, 4):
        column_in = (column + dj >= 0) & (column + dj < CELLS)
        for q in range(-3, 7):
            present[dj + 3, q + 3] = (row_in[q + 3] & column_in).astype(F32)
    spare[0:1, 0:TURNS] = flags[0, 0]
    spare[1:2, 0:TURNS] = flags[0, 1]
    both = spare[...]
    both = jnp.where(lane < TURNS, both, pltpu.roll(both, TURNS, 1))
    no_upper = ply == lax.axis_size("ply") - 1 if not INTERPRET else ply == 7
    for word in range(2):
        plain = jnp.broadcast_to(both[word : word + 1], (8, 128))
        for dj in range(-2, 3):
            column_in = (column + dj >= 0) & (column + dj < CELLS)
            for q in range(8):
                good = row_in[q + 1] & column_in & jnp.logical_not(no_upper)
                words[word, dj + 2, q] = jnp.where(good, plain, -1)
    cos_parts, sin_parts = [], []
    for side in range(2):
        code = codes[0, side]
        cosine = jnp.where(code == 0, 1.0, jnp.where(code == 1, 0.0, ROOT_HALF))
        sine = jnp.where(code == 0, 0.0, jnp.where(code == 1, 1.0, jnp.where(code == 2, ROOT_HALF, -ROOT_HALF)))
        cos_parts.append(jnp.full((8, 128), cosine, F32))
        sin_parts.append(jnp.full((8, 128), sine, F32))
    for place_index, (di, dj) in enumerate(PLANE):
        lean = [(di * cos_parts[side] + dj * sin_parts[side]) ** 2 for side in range(2)]
        if (di, dj) != (0, 0):
            rates[place_index, 0] = coefficient(lean[0], lean[0], 0, di, dj)
            rates[place_index, 1] = coefficient(lean[1], lean[1], 0, di, dj)
        rates[place_index, 2] = coefficient(lean[0], lean[0], 1, di, dj)
        rates[place_index, 3] = coefficient(lean[0], lean[1], 1, di, dj)
        rates[place_index, 4] = coefficient(lean[1], lean[1], 1, di, dj)
        rates[place_index, 5] = coefficient(lean[0], lean[1], 2, di, dj)
    for side in range(2):
        lean = (3 * cos_parts[side]) ** 2
        rates[25, side] = 9.0 * coefficient(lean, lean, 0, 3, 0)
        lean = (3 * sin_parts[side]) ** 2
        rates[25, 2 + side] = 9.0 * coefficient(lean, lean, 0, 0, 3)
    rates[25, 4] = 9.0 * coefficient(jnp.zeros((8, 128), F32), 0.0, 3, 0, 0)

    def bonds(m, carry):
        x = [moved[2, field, m + 3] for field in range(12)]
        total = [None] * 12
        for place_index, (di, dj) in enumerate(PLANE):
            y = [moved[dj + 2, field, m + 3 + di] for field in range(12)]
            far_e = [along(di, dj, y[3 * l], y[3 * l + 1]) for l in range(4)]
            near_e = [along(di, dj, x[3 * l], x[3 * l + 1]) for l in range(4)]
            here = present[dj + 3, m + 3 + di]
            for layer in range(4):
                plane, lift, double = None, None, None
                for other in range(4):
                    dz = other - layer
                    if dz * dz + di * di + dj * dj > 9 or (dz, di, dj) == (0, 0, 0) or abs(dz) == 3:
                        continue
                    pick = {0: layer // 2, 1: 2 + (layer + other) // 2, 2: 5}[abs(dz)]
                    if abs(dz) == 1:
                        pick = 2 + min(layer, other)
                    s = gap(far_e[other], near_e[layer], dz, y[3 * other + 2], x[3 * layer + 2])
                    t = rates[place_index, pick] * s
                    plane = added(plane, t)
                    if abs(dz) == 1:
                        lift = added(lift, t if dz > 0 else -t)
                    if abs(dz) == 2:
                        lift = added(lift, scaled(dz, t))
                if di or dj:
                    plane = plane * here
                    if di:
                        total[3 * layer] = added(total[3 * layer], scaled(di, plane))
                    if dj:
                        total[3 * layer + 1] = added(total[3 * layer + 1], scaled(dj, plane))
                total[3 * layer + 2] = added(total[3 * layer + 2], lift * here)
        rise = rates[25, 4] * (x[11] - x[2])
        total[2] = total[2] + rise
        total[11] = total[11] - rise
        for layer in range(4):
            for side, step in ((0, -3), (1, 3)):
                apart = present[3, m + 3 + step] * (moved[2, 3 * layer, m + 3 + step] - x[3 * layer])
                total[3 * layer] = total[3 * layer] + rates[25, layer // 2] * apart
                apart = present[3 + step, m + 3] * (far[side, layer, m] - x[3 * layer + 1])
                total[3 * layer + 1] = total[3 * layer + 1] + rates[25, 2 + layer // 2] * apart
        for field in range(12):
            force[field, m] = total[field]
        return carry

    lax.fori_loop(0, 4, bonds, 0)


def interface_kernel(message, own, words, force, half, mask, new_v, new_a, facing, moved, below, shared, turned):
    ply, stripe = place()
    cell, lane = lanes_and_cells()
    for q in range(8):
        both = jnp.concatenate(
            [message[pl.ds(q, TURNS, stride=WINDOW), :], message[pl.ds(q + 4, TURNS, stride=WINDOW), :]], axis=0
        )
        facing[q] = both.T
    for q in range(8):
        for slot in range(13):
            if slot == 6:
                continue
            field = facing[q, 8 * slot : 8 * slot + 8]
            moved[2, slot, q] = field
            for dj, other in shifted_by(field, cell)[0].items():
                moved[dj + 2, slot, q] = other
    row = 8 * stripe + jnp.where(lane >= TURNS, 4, 0)
    column = 8 * jnp.bitwise_and(lane, TURNS - 1) + cell
    for source, spots in ((0, (0, 1)), (2, (2, 3, 4, 5)), (6, (6, 7))):
        parts = facing[source, 112:120].astype(I32)
        joined = [jnp.bitwise_or(jnp.left_shift(parts[1:2], 15), parts[0:1]), parts[2:3]]
        for word in range(2):
            plain = jnp.broadcast_to(joined[word], (8, 128))
            before, after = pltpu.roll(plain, 1, 1), pltpu.roll(plain, 127, 1)
            for dj in range(-2, 3):
                turned_word = plain
                if dj < 0:
                    turned_word = jnp.where(cell + dj < 0, before, plain)
                if dj > 0:
                    turned_word = jnp.where(cell + dj > 7, after, plain)
                column_in = (column + dj >= 0) & (column + dj < CELLS) & (ply > 0)
                for q in spots:
                    good = (row + q - 2 >= 0) & (row + q - 2 < CELLS) & column_in
                    below[word, dj + 2, q] = jnp.where(good, turned_word, -1)

    def kept(table, dz, di, dj, spot, column_step):
        k = class_index(dz, di, dj)
        return jnp.bitwise_and(table[k // 30, column_step + 2, spot], 1 << (k % 30)) == 0

    def bonds(m, carry):
        x = [own[field, m] for field in range(12)]
        total = [force[field, m] for field in range(12)]
        for di, dj in PLANE:
            spot = m + 2 + di
            radius = di * di + dj * dj
            y = [moved[dj + 2, slot, spot] if slot != 6 else None for slot in range(13)]
            weight = [0.0] + [INTER_C * RATE / float(dz * dz + radius) ** 1.5 for dz in (1, 2, 3)]
            first = kept(words, 1, di, dj, spot, dj)
            far0, far1 = along(di, dj, y[0], y[1]), along(di, dj, y[3], y[4])
            near3, near2 = along(di, dj, x[9], x[10]), along(di, dj, x[6], x[7])
            t = jnp.where(first, weight[1] * gap(far0, near3, 1, y[2], x[11]), 0.0)
            plane3, lift3 = t, t
            plane2 = None
            if radius <= 5:
                second = kept(words, 2, di, dj, spot, dj)
                t = jnp.where(second, weight[2] * gap(far1, near3, 2, y[5], x[11]), 0.0)
                plane3, lift3 = plane3 + t, lift3 + 2.0 * t
                plane2 = jnp.where(second, weight[2] * gap(far0, near2, 2, y[2], x[8]), 0.0)
            total[11] = total[11] + lift3
            if di:
                total[9] = total[9] + scaled(di, plane3)
            if dj:
                total[10] = total[10] + scaled(dj, plane3)
            if plane2 is not None:
                total[8] = total[8] + 2.0 * plane2
                if di:
                    total[6] = total[6] + scaled(di, plane2)
                if dj:
                    total[7] = total[7] + scaled(dj, plane2)
            first = kept(below, 1, -dj, -di, spot, dj)
            far3, far2 = along(di, dj, y[7], y[8]), along(di, dj, y[10], y[11])
            near0, near1 = along(di, dj, x[0], x[1]), along(di, dj, x[3], x[4])
            t = jnp.where(first, weight[1] * gap(far3, near0, -1, y[9], x[2]), 0.0)
            plane0, lift0 = t, t
            plane1 = None
            if radius <= 5:
                second = kept(below, 2, -dj, -di, spot, dj)
                t = jnp.where(second, weight[2] * gap(far2, near0, -2, y[12], x[2]), 0.0)
                plane0, lift0 = plane0 + t, lift0 + 2.0 * t
                plane1 = jnp.where(second, weight[2] * gap(far3, near1, -2, y[9], x[5]), 0.0)
            total[2] = total[2] - lift0
            if di:
                total[0] = total[0] + scaled(di, plane0)
            if dj:
                total[1] = total[1] + scaled(dj, plane0)
            if plane1 is not None:
                total[5] = total[5] - 2.0 * plane1
                if di:
                    total[3] = total[3] + scaled(di, plane1)
                if dj:
                    total[4] = total[4] + scaled(dj, plane1)
            if radius == 0:
                rise = 9.0 * weight[3]
                third = kept(words, 3, 0, 0, spot, 0)
                top = facing[spot, 48:56]
                total[11] = total[11] + jnp.where(third, rise * (top - x[11]), 0.0)
                total[8] = total[8] + jnp.where(third, rise * (y[5] - x[8]), 0.0)
                total[5] = total[5] + jnp.where(third, rise * (y[2] - x[5]), 0.0)
                third = kept(below, 3, 0, 0, spot, 0)
                bottom = facing[spot, 104:112]
                total[2] = total[2] + jnp.where(third, rise * (bottom - x[2]), 0.0)
                total[5] = total[5] + jnp.where(third, rise * (y[12] - x[5]), 0.0)
                total[8] = total[8] + jnp.where(third, rise * (y[9] - x[8]), 0.0)
        for field in range(12):
            shared[8 * field + m] = total[field]
            shared[8 * field + 4 + m] = total[field]
        return carry

    lax.fori_loop(0, 4, bonds, 0)
    flat = shared.reshape(96 * 8, 128)
    low_row = jnp.bitwise_and(lax.broadcasted_iota(I32, (TURNS, 96), 1), 7) < 4
    for position in range(8):
        both = flat[pl.ds(position, 96, stride=8), :].T
        turned[pl.ds(position, TURNS, stride=8), 0:96] = jnp.where(low_row, both[0:TURNS], both[TURNS:])
    top = (ply == (lax.axis_size("ply") if not INTERPRET else 8) - 1).astype(F32)
    for piece in range(4):
        columns = slice(128 * piece, 128 * piece + 128)
        back = turned[columns, :].T
        for layer in range(4):
            for comp in range(3):
                field = 3 * layer + comp
                value = back[8 * field : 8 * field + 8]
                if field == 11:
                    value = value - (IMPACT * top) * mask[:, columns].astype(F32)
                new_a[comp, 0, layer, :, columns] = value
                new_v[comp, 0, layer, :, columns] = half[comp, 0, layer, :, columns] + 0.5 * value


def shape(*dims, dtype=F32):
    return jax.ShapeDtypeStruct(dims, dtype)


def run_advance(displacement, velocity, acceleration, flags):
    return pl.pallas_call(
        advance_kernel,
        out_shape=(
            shape(3, 1, 4, ROWS, CELLS),
            shape(3, 1, 4, ROWS, CELLS),
            shape(56, CELLS),
            shape(64, CELLS),
            shape(12, 3, CELLS),
            shape(12, 3, CELLS),
        ),
        interpret=INTERPRET,
    )(displacement, velocity, acceleration, flags)


def run_turn(above, below):
    call = kernel_call(turn_kernel, shape(TURNS * WINDOW, 128), [pltpu.VMEM((CELLS + 16, 128), F32)], 1_000_000)
    return call(above, below)


def run_pair(adv, low, high, codes, flags):
    vmem = pl.BlockSpec(memory_space=pltpu.VMEM)
    return pl.pallas_call(
        pair_kernel,
        out_shape=(shape(12, 4, 8, 128), shape(12, 4, 8, 128), shape(2, 5, 8, 8, 128, dtype=I32)),
        in_specs=[vmem, vmem, vmem, pl.BlockSpec(memory_space=pltpu.SMEM), vmem],
        scratch_shapes=[
            pltpu.VMEM((2, 128, CELLS), F32),
            pltpu.VMEM((2, CELLS, 128), F32),
            pltpu.VMEM((8 * 128, 128), F32),
            pltpu.VMEM((5, 12, 10, 8, 128), F32),
            pltpu.VMEM((2, 4, 4, 8, 128), F32),
            pltpu.VMEM((26, 6, 8, 128), F32),
            pltpu.VMEM((7, 10, 8, 128), F32),
            pltpu.VMEM((8, 128), I32),
        ],
        interpret=INTERPRET,
        cost_estimate=pl.CostEstimate(flops=50_000_000, bytes_accessed=2_000_000, transcendentals=0),
    )(adv, low, high, codes, flags)


def run_interface(message, own, words, force, half, mask):
    return pl.pallas_call(
        interface_kernel,
        out_shape=(shape(3, 1, 4, ROWS, CELLS), shape(3, 1, 4, ROWS, CELLS)),
        scratch_shapes=[
            pltpu.VMEM((8, 128, 128), F32),
            pltpu.VMEM((5, 13, 8, 8, 128), F32),
            pltpu.VMEM((2, 5, 8, 8, 128), I32),
            pltpu.VMEM((96, 8, 128), F32),
            pltpu.VMEM((CELLS, 128), F32),
        ],
        interpret=INTERPRET,
    )(message, own, words, force, half, mask)


def steps(axis, by):
    count = lax.axis_size(axis)
    return [(i, i + by) for i in range(count) if 0 <= i + by < count]


def local(displacement, velocity, acceleration, fibre_codes, contact_mask, bond_flags):
    adv, half, down, up, low, high = run_advance(displacement, velocity, acceleration, bond_flags)
    above = lax.ppermute(down, "ply", steps("ply", -1))
    below = lax.ppermute(up, "ply", steps("ply", 1))
    low = lax.ppermute(low, "stripe", steps("stripe", 1))
    high = lax.ppermute(high, "stripe", steps("stripe", -1))
    message = run_turn(above, below).reshape(TURNS, 1, WINDOW * 128)
    message = lax.all_to_all(message, "stripe", 0, 0).reshape(TURNS * WINDOW, 128)
    force, own, words = run_pair(adv, low, high, fibre_codes, bond_flags)
    new_velocity, new_acceleration = run_interface(message, own, words, force, half, contact_mask)
    return adv, new_velocity, new_acceleration


def solution(mesh):
    state = P(None, "ply", None, "stripe", None)
    return jax.shard_map(
        local,
        mesh=mesh,
        in_specs=(state, state, state, P("ply", None), P("stripe", None), P("ply", None, "stripe", None)),
        out_specs=(state, state, state),
        check_vma=False,
    )
```

```python
import jax
import jax.numpy as jnp
from jax import lax
from jax.experimental import pallas as pl
from jax.experimental.pallas import tpu as pltpu
from jax.sharding import PartitionSpec as P


ROOT_HALF = 0.7071067811865476
RATE = 0.025
MATRIX_C = 1.0
FIBRE_C = 4.0
INTER_C = 1.5
IMPACT = 2.0

F32 = jnp.float32
I32 = jnp.int32
ROWS = 8
TURNS = 64
CELLS = ROWS * TURNS
WINDOW = 11
SPREAD = [(2, 0), (3, 16), (4, 32), (5, 56), (6, 72), (7, 88)]
PLANE = [(di, dj) for di in range(-2, 3) for dj in range(-2, 3)]
INTERPRET = False


def place():
    return lax.axis_index("ply"), lax.axis_index("stripe")


def class_index(dz, di, dj):
    count = 0
    for z in range(1, 4):
        for i in range(-3, 4):
            for j in range(-3, 4):
                if z * z + i * i + j * j <= 9:
                    if (z, i, j) == (dz, di, dj):
                        return count
                    count += 1
    raise ValueError("no class")


def scaled(factor, value):
    if factor == 1:
        return value
    if factor == -1:
        return -value
    return factor * value


def along(di, dj, first, second):
    if di == 0 and dj == 0:
        return None
    if di == 0:
        return scaled(dj, second)
    if dj == 0:
        return scaled(di, first)
    if abs(di) == abs(dj):
        inner = first + second if di == dj else first - second
        return scaled(di, inner)
    return scaled(di, first) + scaled(dj, second)


def gap(far, near, rise, far_z, near_z):
    total = None if far is None else far - near
    if rise:
        lift = scaled(rise, far_z - near_z)
        total = lift if total is None else total + lift
    return total


def added(total, value):
    return value if total is None else total + value


def lanes_and_cells():
    cell = lax.broadcasted_iota(I32, (8, 128), 0)
    lane = lax.broadcasted_iota(I32, (8, 128), 1)
    return cell, lane


def shifted_by(value, cell):
    after = pltpu.roll(value, 127, 1)
    before = pltpu.roll(value, 1, 1)
    moved = {}
    for dj in (1, 2):
        moved[dj] = pltpu.roll(jnp.where(cell < dj, after, value), 8 - dj, 0)
        moved[-dj] = pltpu.roll(jnp.where(cell >= 8 - dj, before, value), dj, 0)
    return moved, after, before


def advance_kernel(disp, vel, acc, flags, adv, half, down, up, low, high):
    values = []
    for layer in range(4):
        for comp in range(3):
            speed = vel[comp, 0, layer] + 0.5 * acc[comp, 0, layer]
            moved = disp[comp, 0, layer] + speed
            half[comp, 0, layer] = speed
            adv[comp, 0, layer] = moved
            field = 3 * layer + comp
            low[3 * field : 3 * field + 3] = moved[5:8]
            high[3 * field : 3 * field + 3] = moved[0:3]
            values.append(moved)
    low[36:40] = jnp.zeros((4, CELLS), F32)
    high[36:40] = jnp.zeros((4, CELLS), F32)
    for slot, field in enumerate((1, 0, 2, 4, 3, 5, 8)):
        down[8 * slot : 8 * slot + 8] = values[field]
    for slot, field in enumerate((10, 9, 11, 7, 6, 8, 5)):
        up[8 * slot : 8 * slot + 8] = values[field]
    first = flags[0, 0]
    second = flags[0, 1]
    parts = jnp.concatenate(
        [jnp.bitwise_and(first, 0x7FFF), jnp.right_shift(first, 15), second, jnp.zeros((5, TURNS), I32)],
        axis=0,
    ).astype(F32)
    block = lax.broadcasted_iota(I32, (TURNS, CELLS), 0)
    column = lax.broadcasted_iota(I32, (TURNS, CELLS), 1)
    spread = (jnp.right_shift(column, 3) == block).astype(F32)
    up[56:64] = jnp.dot(parts, spread, precision=lax.Precision.HIGHEST, preferred_element_type=F32)


def turn_kernel(above, below, message, turned):
    stacked = jnp.concatenate([above[...], below[...], jnp.zeros((8, CELLS), F32)], axis=0)
    turned[0:8] = jnp.zeros((8, 128), F32)
    turned[CELLS + 8 : CELLS + 16] = jnp.zeros((8, 128), F32)
    for piece in range(4):
        turned[8 + 128 * piece : 136 + 128 * piece] = stacked[:, 128 * piece : 128 * piece + 128].T
    lane = lax.broadcasted_iota(I32, (TURNS, 128), 1)
    last = turned[pl.ds(17, TURNS, stride=8), :]
    starts = dict(SPREAD)
    for row in range(WINDOW):
        line = turned[pl.ds(6 + row, TURNS, stride=8), :]
        if row in starts:
            line = jnp.where(lane < 112, line, pltpu.roll(last, 112 - starts[row], 1))
        message[pl.ds(row, TURNS, stride=WINDOW), :] = line


def coefficient(here, there, dz, di, dj):
    radius = float(dz * dz + di * di + dj * dj)
    level = RATE / radius**1.5
    return level * MATRIX_C + (level * FIBRE_C * 0.5 / radius) * (here + there)


def pair_bonds(di, dj, x, y, here, rate, total):
    far_e = [along(di, dj, y[3 * l], y[3 * l + 1]) for l in range(4)]
    near_e = [along(di, dj, x[3 * l], x[3 * l + 1]) for l in range(4)]
    for layer in range(4):
        plane, lift = None, None
        for other in range(4):
            dz = other - layer
            if dz * dz + di * di + dj * dj > 9 or (dz, di, dj) == (0, 0, 0) or abs(dz) == 3:
                continue
            pick = (layer // 2, 2 + min(layer, other), 5)[abs(dz)]
            s = gap(far_e[other], near_e[layer], dz, y[3 * other + 2], x[3 * layer + 2])
            t = rate(pick) * s
            plane = added(plane, t)
            if abs(dz) == 1:
                lift = added(lift, t if dz > 0 else -t)
            if abs(dz) == 2:
                lift = added(lift, scaled(dz, t))
        if di or dj:
            plane = plane * here
            if di:
                total[3 * layer] = added(total[3 * layer], scaled(di, plane))
            if dj:
                total[3 * layer + 1] = added(total[3 * layer + 1], scaled(dj, plane))
        total[3 * layer + 2] = added(total[3 * layer + 2], lift * here)


def pair_kernel(adv, codes, flags, mask, force, base, strengths, rates, present, impact, turned, held, moved, far, spare):
    ply, stripe = place()
    cell, lane = lanes_and_cells()
    for side in range(2):
        rows = []
        for field in range(12):
            whole = adv[field % 3, 0, field // 3]
            rows.append(whole if side == 0 else pltpu.roll(whole, 4, 0))
        stacked = jnp.concatenate(rows, axis=0)
        for piece in range(4):
            turned[side, 128 * piece : 128 * piece + 128, 0:96] = stacked[:, 128 * piece : 128 * piece + 128].T
    for position in range(8):
        pick = pl.ds(position, TURNS, stride=8)
        both = jnp.concatenate([turned[0, pick, :], turned[1, pick, :]], axis=0)
        held[96 * position : 96 * position + 96] = both.T[0:96]
    for field in range(12):
        for q in range(8):
            value = held[pl.ds(8 * field + q, 8, stride=96), :]
            base[field, q] = value
            if q < 4:
                others, after, before = shifted_by(value, cell)
                for dj, other in others.items():
                    moved[dj + 2, field, q] = other
                if field % 3 == 1:
                    far[0, field // 3, q] = pltpu.roll(jnp.where(cell >= 5, before, value), 3, 0)
                    far[1, field // 3, q] = pltpu.roll(jnp.where(cell < 3, after, value), 5, 0)
    row = 8 * stripe + jnp.where(lane >= TURNS, 4, 0)
    column = 8 * jnp.bitwise_and(lane, TURNS - 1) + cell
    row_in = [(row + q >= 0) & (row + q < CELLS) for q in range(-3, 7)]
    for dj in range(-3, 4):
        column_in = (column + dj >= 0) & (column + dj < CELLS)
        for q in range(-3, 7):
            present[dj + 3, q + 3] = (row_in[q + 3] & column_in).astype(F32)
    spare[0:1, 0:TURNS] = flags[0, 0]
    spare[1:2, 0:TURNS] = flags[0, 1]
    both = spare[...]
    both = jnp.where(lane < TURNS, both, pltpu.roll(both, TURNS, 1))
    plain = [jnp.broadcast_to(both[word : word + 1], (8, 128)) for word in range(2)]
    top = ply == (lax.axis_size("ply") if not INTERPRET else 8) - 1
    lower = jnp.where(top, 0.0, 1.0)
    for spot, (di, dj) in enumerate(PLANE):
        for dz in (1, 2, 3):
            if dz * dz + di * di + dj * dj <= 9:
                k = class_index(dz, di, dj)
                whole = jnp.bitwise_and(plain[k // 30], 1 << (k % 30)) == 0
                strength = jnp.where(whole, lower * weight(dz, di, dj), 0.0)
                for m in range(4):
                    strengths[dz - 1 if dz < 3 else 0, spot if dz < 3 else 25, m] = strength * present[dj + 3, m + di + 3]
    impact[...] = (IMPACT * top.astype(F32)) * mask[...].astype(F32)
    cos_parts, sin_parts = [], []
    for side in range(2):
        code = codes[0, side]
        cosine = jnp.where(code == 0, 1.0, jnp.where(code == 1, 0.0, ROOT_HALF))
        sine = jnp.where(code == 0, 0.0, jnp.where(code == 1, 1.0, jnp.where(code == 2, ROOT_HALF, -ROOT_HALF)))
        cos_parts.append(jnp.full((8, 128), cosine, F32))
        sin_parts.append(jnp.full((8, 128), sine, F32))
    for spot, (di, dj) in enumerate(PLANE):
        lean = [(di * cos_parts[side] + dj * sin_parts[side]) ** 2 for side in range(2)]
        if (di, dj) != (0, 0):
            rates[spot, 0] = coefficient(lean[0], lean[0], 0, di, dj)
            rates[spot, 1] = coefficient(lean[1], lean[1], 0, di, dj)
        rates[spot, 2] = coefficient(lean[0], lean[0], 1, di, dj)
        rates[spot, 3] = coefficient(lean[0], lean[1], 1, di, dj)
        rates[spot, 4] = coefficient(lean[1], lean[1], 1, di, dj)
        rates[spot, 5] = coefficient(lean[0], lean[1], 2, di, dj)
    for side in range(2):
        lean = (3 * cos_parts[side]) ** 2
        rates[25, side] = 9.0 * coefficient(lean, lean, 0, 3, 0)
        lean = (3 * sin_parts[side]) ** 2
        rates[25, 2 + side] = 9.0 * coefficient(lean, lean, 0, 0, 3)
    rates[25, 4] = 9.0 * coefficient(jnp.zeros((8, 128), F32), 0.0, 3, 0, 0)
    for m in range(4):
        x = [base[field, m] for field in range(12)]
        rise = rates[25, 4] * (x[11] - x[2])
        total = [None] * 12
        total[2], total[11] = rise, -rise
        for spot, (di, dj) in enumerate(PLANE):
            q = m + di
            if 0 <= q < 4:
                y = [moved[dj + 2, field, q] if dj else base[field, q] for field in range(12)]
                pair_bonds(di, dj, x, y, present[dj + 3, q + 3], lambda pick: rates[spot, pick], total)
        for layer in range(4):
            for step in (-3, 3):
                if 0 <= m + step < 4:
                    apart = base[3 * layer, m + step] - x[3 * layer]
                    total[3 * layer] = added(total[3 * layer], rates[25, layer // 2] * apart)
            for side, step in ((0, -3), (1, 3)):
                apart = present[3 + step, m + 3] * (far[side, layer, m] - x[3 * layer + 1])
                total[3 * layer + 1] = total[3 * layer + 1] + rates[25, 2 + layer // 2] * apart
        for field in range(12):
            force[field, m] = total[field]


def weight(dz, di, dj):
    return INTER_C * RATE / float(dz * dz + di * di + dj * dj) ** 1.5


EDGE_ROWS = (-2, -1, 4, 5)


def edge_kernel(low, high, base, rates, present, partial, force, turned, held, moved):
    cell, lane = lanes_and_cells()
    left = lane < TURNS
    for side, rows in enumerate((low, high)):
        for piece in range(4):
            turned[side, 128 * piece : 128 * piece + 128, 0:40] = rows[:, 128 * piece : 128 * piece + 128].T
    for position in range(8):
        pick = pl.ds(position, TURNS, stride=8)
        both = jnp.concatenate([turned[0, pick, :], turned[1, pick, :]], axis=0)
        held[40 * position : 40 * position + 40] = both.T[0:40]

    def around(field, q):
        other = held[pl.ds(3 * field + (q + 3 if q < 0 else q - 4), 8, stride=40), :]
        return jnp.where(left, other, base[field, q + 8]) if q < 0 else jnp.where(left, base[field, q], other)

    for field in range(12):
        for spot, q in enumerate(EDGE_ROWS):
            value = around(field, q)
            moved[2, field, spot] = value
            for dj, other in shifted_by(value, cell)[0].items():
                moved[dj + 2, field, spot] = other
    for m in range(4):
        x = [base[field, m] for field in range(12)]
        total = [partial[field, m] for field in range(12)]
        for spot, (di, dj) in enumerate(PLANE):
            q = m + di
            if q in EDGE_ROWS:
                y = [moved[dj + 2, field, EDGE_ROWS.index(q)] for field in range(12)]
                pair_bonds(di, dj, x, y, present[dj + 3, q + 3], lambda pick: rates[spot, pick], total)
        for layer in range(4):
            for q in (m - 3, m + 3):
                if q < 0 or q > 3:
                    apart = present[3, q + 3] * (around(3 * layer, q) - x[3 * layer])
                    total[3 * layer] = total[3 * layer] + rates[25, layer // 2] * apart
        for field in range(12):
            force[field, m] = total[field]


def grown(sums, key, sign, value):
    if key not in sums:
        sums[key] = value if sign > 0 else -value
    else:
        sums[key] = sums[key] + value if sign > 0 else sums[key] - value


def stretched(turn, far, near, rise, far_z, near_z):
    lift = far_z - near_z
    if abs(rise) == 2:
        lift = lift + lift
    if far is None:
        return lift, 1 if rise > 0 else -1
    core = far - near
    if rise > 0:
        return (core + lift if turn > 0 else lift - core), 1
    return (core - lift, 1) if turn > 0 else (core + lift, -1)


def pushed(sums, wide, field, di, dj, sign, value):
    for step, spot in ((di, field), (dj, field + 1)):
        if step:
            grown(sums if abs(step) == 1 else wide, spot, sign if step > 0 else -sign, value)


def interface_kernel(message, own, strengths, force, half, impact, new_v, new_a, facing, moved, below, shared, turned):
    ply, stripe = place()
    cell, lane = lanes_and_cells()
    wide_lane = lax.broadcasted_iota(I32, (TURNS, 128), 1)
    lines = [message[pl.ds(row, TURNS, stride=WINDOW), :] for row in range(WINDOW)]
    last = lines[0]
    for row, start in SPREAD:
        last = jnp.where(wide_lane < start, last, pltpu.roll(lines[row], start + 16, 1))
    lines.append(last)
    for q in range(8):
        facing[q] = jnp.concatenate([lines[q], lines[q + 4]], axis=0).T
    row = 8 * stripe + jnp.where(lane >= TURNS, 4, 0)
    column = 8 * jnp.bitwise_and(lane, TURNS - 1) + cell
    left = lane < TURNS
    same = facing[4, 112:120]
    twin = pltpu.roll(same, TURNS, 1)
    for parts, spots in (
        (jnp.where(left, facing[0, 112:120], same), (0, 1)),
        (jnp.where(left, twin, same), (2, 3, 4, 5)),
        (jnp.where(left, twin, facing[6, 112:120]), (6, 7)),
    ):
        parts = parts.astype(I32)
        joined = [jnp.bitwise_or(jnp.left_shift(parts[1:2], 15), parts[0:1]), parts[2:3]]
        for word in range(2):
            plain = jnp.broadcast_to(joined[word], (8, 128))
            before, after = pltpu.roll(plain, 1, 1), pltpu.roll(plain, 127, 1)
            for dj in range(-2, 3):
                turned_word = plain
                if dj < 0:
                    turned_word = jnp.where(cell + dj < 0, before, plain)
                if dj > 0:
                    turned_word = jnp.where(cell + dj > 7, after, plain)
                column_in = (column + dj >= 0) & (column + dj < CELLS) & (ply > 0)
                for q in spots:
                    good = (row + q - 2 >= 0) & (row + q - 2 < CELLS) & column_in
                    below[word, dj + 2, q] = jnp.where(good, turned_word, -1)

    def spread(q):
        for slot in (0, 1, 2, 3, 4, 5, 7, 8, 9, 10, 11, 12):
            field = facing[q, 8 * slot : 8 * slot + 8]
            for dj, other in shifted_by(field, cell)[0].items():
                moved[dj + 2, slot, q] = other

    def kept(dz, di, dj, spot, value):
        k = class_index(dz, -dj, -di)
        whole = jnp.bitwise_and(below[k // 30, dj + 2, spot], 1 << (k % 30)) == 0
        return jnp.where(whole, weight(dz, di, dj) * value, 0.0)

    def bonds(m):
        x = [own[field, m] for field in range(12)]
        sums = {field: force[field, m] for field in range(12)}
        wide, double = {}, {}
        for spot, (di, dj) in enumerate(PLANE):
            q = m + 2 + di
            close = di * di + dj * dj <= 5
            turn = 1 if (di, dj) >= (0, 0) else -1
            pi, pj = turn * di, turn * dj

            def y(slot):
                return moved[dj + 2, slot, q] if dj else facing[q, 8 * slot : 8 * slot + 8]

            far, far_z = along(pi, pj, y(0), y(1)), y(2)
            near = along(pi, pj, x[9], x[10])
            value, sign = stretched(turn, far, near, 1, far_z, x[11])
            first = strengths[0, spot, m] * value
            grown(sums, 11, sign, first)
            plane = first
            if close:
                value, sign = stretched(turn, along(pi, pj, y(3), y(4)), near, 2, y(5), x[11])
                second = strengths[1, spot, m] * value
                grown(double, 11, sign, second)
                plane = first + second
                value, sign = stretched(turn, far, along(pi, pj, x[6], x[7]), 2, far_z, x[8])
                second = strengths[1, spot, m] * value
                grown(double, 8, sign, second)
                pushed(sums, wide, 6, di, dj, sign, second)
            pushed(sums, wide, 9, di, dj, sign, plane)
            far, far_z = along(pi, pj, y(7), y(8)), y(9)
            near = along(pi, pj, x[0], x[1])
            value, sign = stretched(turn, far, near, -1, far_z, x[2])
            first = kept(1, di, dj, q, value)
            grown(sums, 2, -sign, first)
            plane = first
            if close:
                value, sign = stretched(turn, along(pi, pj, y(10), y(11)), near, -2, y(12), x[2])
                second = kept(2, di, dj, q, value)
                grown(double, 2, -sign, second)
                plane = first + second
                value, sign = stretched(turn, far, along(pi, pj, x[3], x[4]), -2, far_z, x[5])
                second = kept(2, di, dj, q, value)
                grown(double, 5, -sign, second)
                pushed(sums, wide, 3, di, dj, sign, second)
            pushed(sums, wide, 0, di, dj, sign, plane)
            if di == 0 and dj == 0:
                rise = 9.0 * strengths[0, 25, m]
                grown(sums, 11, 1, rise * (facing[q, 48:56] - x[11]))
                grown(sums, 8, 1, rise * (y(5) - x[8]))
                grown(sums, 5, 1, rise * (y(2) - x[5]))
                grown(sums, 2, 1, kept(3, 0, 0, q, 9.0 * (facing[q, 104:112] - x[2])))
                grown(sums, 5, 1, kept(3, 0, 0, q, 9.0 * (y(12) - x[5])))
                grown(sums, 8, 1, kept(3, 0, 0, q, 9.0 * (y(9) - x[8])))
        for extra in (wide, double):
            for field, value in extra.items():
                sums[field] = sums[field] + 2.0 * value
        for field in range(12):
            shared[8 * field + m] = sums[field]
            shared[8 * field + 4 + m] = sums[field]

    for q in range(4):
        spread(q)
    for m in range(4):
        spread(m + 4)
        bonds(m)
    flat = shared.reshape(96 * 8, 128)
    low_row = jnp.bitwise_and(lax.broadcasted_iota(I32, (TURNS, 96), 1), 7) < 4
    for position in range(8):
        both = flat[pl.ds(position, 96, stride=8), :].T
        turned[pl.ds(position, TURNS, stride=8), 0:96] = jnp.where(low_row, both[0:TURNS], both[TURNS:])
    for piece in range(4):
        columns = slice(128 * piece, 128 * piece + 128)
        back = turned[columns, :].T
        for layer in range(4):
            for comp in range(3):
                field = 3 * layer + comp
                value = back[8 * field : 8 * field + 8]
                if field == 11:
                    value = value - impact[:, columns]
                new_a[comp, 0, layer, :, columns] = value
                new_v[comp, 0, layer, :, columns] = half[comp, 0, layer, :, columns] + 0.5 * value


def shape(*dims, dtype=F32):
    return jax.ShapeDtypeStruct(dims, dtype)


def near(*dims, dtype=F32):
    return shape(*dims, dtype=dtype) if INTERPRET else pltpu.VMEM(dims, dtype)


def kept_near(array):
    return array if INTERPRET else pltpu.with_memory_space_constraint(array, pltpu.VMEM)


def run_advance(displacement, velocity, acceleration, flags):
    return pl.pallas_call(
        advance_kernel,
        out_shape=(
            near(3, 1, 4, ROWS, CELLS),
            near(3, 1, 4, ROWS, CELLS),
            near(56, CELLS),
            near(64, CELLS),
            near(40, CELLS),
            near(40, CELLS),
        ),
        interpret=INTERPRET,
    )(displacement, velocity, acceleration, flags)


def run_turn(above, below):
    return pl.pallas_call(
        turn_kernel,
        out_shape=near(TURNS * WINDOW, 128),
        scratch_shapes=[pltpu.VMEM((CELLS + 16, 128), F32)],
        interpret=INTERPRET,
        compiler_params=pltpu.CompilerParams(vmem_limit_bytes=16 * 1024 * 1024),
    )(kept_near(above), kept_near(below))


def run_pair(adv, codes, flags, mask):
    vmem = pl.BlockSpec(memory_space=pltpu.VMEM)
    return pl.pallas_call(
        pair_kernel,
        out_shape=(
            near(12, 4, 8, 128),
            near(12, 8, 8, 128),
            near(2, 26, 4, 8, 128),
            near(26, 6, 8, 128),
            near(7, 10, 8, 128),
            near(8, CELLS),
        ),
        in_specs=[vmem, pl.BlockSpec(memory_space=pltpu.SMEM), vmem, vmem],
        scratch_shapes=[
            pltpu.VMEM((2, CELLS, 128), F32),
            pltpu.VMEM((8 * 96, 128), F32),
            pltpu.VMEM((5, 12, 4, 8, 128), F32),
            pltpu.VMEM((2, 4, 4, 8, 128), F32),
            pltpu.VMEM((8, 128), I32),
        ],
        interpret=INTERPRET,
        compiler_params=pltpu.CompilerParams(vmem_limit_bytes=16 * 1024 * 1024),
        cost_estimate=pl.CostEstimate(flops=20_000_000, bytes_accessed=1_000_000, transcendentals=0),
    )(kept_near(adv), codes, flags, mask)


def run_edge(low, high, base, rates, present, partial):
    return pl.pallas_call(
        edge_kernel,
        out_shape=near(12, 4, 8, 128),
        scratch_shapes=[
            pltpu.VMEM((2, CELLS, 128), F32),
            pltpu.VMEM((8 * 40, 128), F32),
            pltpu.VMEM((5, 12, 4, 8, 128), F32),
        ],
        interpret=INTERPRET,
        compiler_params=pltpu.CompilerParams(vmem_limit_bytes=16 * 1024 * 1024),
        cost_estimate=pl.CostEstimate(flops=10_000_000, bytes_accessed=1_000_000, transcendentals=0),
    )(*[kept_near(array) for array in (low, high, base, rates, present, partial)])


def run_interface(message, own, strengths, force, half, impact):
    return pl.pallas_call(
        interface_kernel,
        out_shape=(shape(3, 1, 4, ROWS, CELLS), shape(3, 1, 4, ROWS, CELLS)),
        scratch_shapes=[
            pltpu.VMEM((8, 128, 128), F32),
            pltpu.VMEM((5, 13, 8, 8, 128), F32),
            pltpu.VMEM((2, 5, 8, 8, 128), I32),
            pltpu.VMEM((96, 8, 128), F32),
            pltpu.VMEM((CELLS, 128), F32),
        ],
        interpret=INTERPRET,
        compiler_params=pltpu.CompilerParams(vmem_limit_bytes=16 * 1024 * 1024),
    )(kept_near(message), kept_near(own), kept_near(strengths), kept_near(force), kept_near(half), kept_near(impact))


def steps(axis, by):
    count = lax.axis_size(axis)
    return [(i, i + by) for i in range(count) if 0 <= i + by < count]


def local(displacement, velocity, acceleration, fibre_codes, contact_mask, bond_flags):
    adv, half, down, up, low, high = run_advance(displacement, velocity, acceleration, bond_flags)
    above = lax.ppermute(down, "ply", steps("ply", -1))
    below = lax.ppermute(up, "ply", steps("ply", 1))
    low = lax.ppermute(low, "stripe", steps("stripe", 1))
    high = lax.ppermute(high, "stripe", steps("stripe", -1))
    message = run_turn(above, below).reshape(TURNS, 1, WINDOW * 128)
    message = lax.all_to_all(message, "stripe", 0, 0)
    partial, own, strengths, rates, present, impact = run_pair(adv, fibre_codes, bond_flags, contact_mask)
    force = run_edge(low, high, own, rates, present, partial)
    message = message.reshape(TURNS * WINDOW, 128)
    new_velocity, new_acceleration = run_interface(message, own, strengths, force, half, impact)
    return adv, new_velocity, new_acceleration


def solution(mesh):
    state = P(None, "ply", None, "stripe", None)
    return jax.shard_map(
        local,
        mesh=mesh,
        in_specs=(state, state, state, P("ply", None), P("stripe", None), P("ply", None, "stripe", None)),
        out_specs=(state, state, state),
        check_vma=False,
    )
```

```python
import jax
import jax.numpy as jnp
from jax import lax
from jax.experimental import pallas as pl
from jax.experimental.pallas import tpu as pltpu
from jax.sharding import PartitionSpec as P


ROOT_HALF = 0.7071067811865476
RATE = 0.025
MATRIX_C = 1.0
FIBRE_C = 4.0
INTER_C = 1.5
IMPACT = 2.0

F32 = jnp.float32
I32 = jnp.int32
ROWS = 8
TURNS = 64
CELLS = ROWS * TURNS
WINDOW = 11
SPREAD = [(2, 0), (3, 16), (4, 32), (5, 56), (6, 72), (7, 88)]
PLANE = [(di, dj) for di in range(-2, 3) for dj in range(-2, 3)]
INTERPRET = False


def place():
    return lax.axis_index("ply"), lax.axis_index("stripe")


def class_index(dz, di, dj):
    count = 0
    for z in range(1, 4):
        for i in range(-3, 4):
            for j in range(-3, 4):
                if z * z + i * i + j * j <= 9:
                    if (z, i, j) == (dz, di, dj):
                        return count
                    count += 1
    raise ValueError("no class")


def scaled(factor, value):
    if factor == 1:
        return value
    if factor == -1:
        return -value
    return factor * value


def along(di, dj, first, second):
    if di == 0 and dj == 0:
        return None
    if di == 0:
        return scaled(dj, second)
    if dj == 0:
        return scaled(di, first)
    if abs(di) == abs(dj):
        inner = first + second if di == dj else first - second
        return scaled(di, inner)
    return scaled(di, first) + scaled(dj, second)


def gap(far, near, rise, far_z, near_z):
    total = None if far is None else far - near
    if rise:
        lift = scaled(rise, far_z - near_z)
        total = lift if total is None else total + lift
    return total


def added(total, value):
    return value if total is None else total + value


def lanes_and_cells():
    cell = lax.broadcasted_iota(I32, (8, 128), 0)
    lane = lax.broadcasted_iota(I32, (8, 128), 1)
    return cell, lane


def shifted_by(value, cell):
    after = pltpu.roll(value, 127, 1)
    before = pltpu.roll(value, 1, 1)
    moved = {}
    for dj in (1, 2):
        moved[dj] = pltpu.roll(jnp.where(cell < dj, after, value), 8 - dj, 0)
        moved[-dj] = pltpu.roll(jnp.where(cell >= 8 - dj, before, value), dj, 0)
    return moved, after, before


def advance_kernel(disp, vel, acc, flags, adv, half, one, two, low, high):
    values = []
    for layer in range(4):
        for comp in range(3):
            speed = vel[comp, 0, layer] + 0.5 * acc[comp, 0, layer]
            moved = disp[comp, 0, layer] + speed
            half[comp, 0, layer] = speed
            adv[comp, 0, layer] = moved
            field = 3 * layer + comp
            low[3 * field : 3 * field + 3] = moved[5:8]
            high[3 * field : 3 * field + 3] = moved[0:3]
            values.append(moved)
    low[36:40] = jnp.zeros((4, CELLS), F32)
    high[36:40] = jnp.zeros((4, CELLS), F32)
    even = jnp.bitwise_and(place()[0], 1) == 0
    for slot, fields in enumerate(zip((1, 0, 2, 4, 3, 5, 8), (10, 9, 11, 7, 6, 8, 5))):
        to_lower, to_upper = (values[field] for field in fields)
        one[8 * slot : 8 * slot + 8] = jnp.where(even, to_upper, to_lower)
        two[8 * slot : 8 * slot + 8] = jnp.where(even, to_lower, to_upper)
    first = flags[0, 0]
    second = flags[0, 1]
    parts = jnp.concatenate(
        [jnp.bitwise_and(first, 0x7FFF), jnp.right_shift(first, 15), second, jnp.zeros((5, TURNS), I32)],
        axis=0,
    ).astype(F32)
    block = lax.broadcasted_iota(I32, (TURNS, CELLS), 0)
    column = lax.broadcasted_iota(I32, (TURNS, CELLS), 1)
    spread = (jnp.right_shift(column, 3) == block).astype(F32)
    spread_parts = jnp.dot(parts, spread, precision=lax.Precision.HIGHEST, preferred_element_type=F32)
    one[56:64] = spread_parts
    two[56:64] = spread_parts


def turn_kernel(one, two, message, turned):
    even = jnp.bitwise_and(place()[0], 1) == 0
    first, second = one[...], two[...]
    above = jnp.where(even, first[0:56], second[0:56])
    below = jnp.where(even, second, first)
    stacked = jnp.concatenate([above, below, jnp.zeros((8, CELLS), F32)], axis=0)
    turned[0:8] = jnp.zeros((8, 128), F32)
    turned[CELLS + 8 : CELLS + 16] = jnp.zeros((8, 128), F32)
    for piece in range(4):
        turned[8 + 128 * piece : 136 + 128 * piece] = stacked[:, 128 * piece : 128 * piece + 128].T
    lane = lax.broadcasted_iota(I32, (TURNS, 128), 1)
    last = turned[pl.ds(17, TURNS, stride=8), :]
    starts = dict(SPREAD)
    for row in range(WINDOW):
        line = turned[pl.ds(6 + row, TURNS, stride=8), :]
        if row in starts:
            line = jnp.where(lane < 112, line, pltpu.roll(last, 112 - starts[row], 1))
        message[pl.ds(row, TURNS, stride=WINDOW), :] = line


def coefficient(here, there, dz, di, dj):
    radius = float(dz * dz + di * di + dj * dj)
    level = RATE / radius**1.5
    return level * MATRIX_C + (level * FIBRE_C * 0.5 / radius) * (here + there)


def pair_bonds(di, dj, x, y, here, rate, total):
    far_e = [along(di, dj, y[3 * l], y[3 * l + 1]) for l in range(4)]
    near_e = [along(di, dj, x[3 * l], x[3 * l + 1]) for l in range(4)]
    for layer in range(4):
        plane, lift = None, None
        for other in range(4):
            dz = other - layer
            if dz * dz + di * di + dj * dj > 9 or (dz, di, dj) == (0, 0, 0) or abs(dz) == 3:
                continue
            pick = (layer // 2, 2 + min(layer, other), 5)[abs(dz)]
            s = gap(far_e[other], near_e[layer], dz, y[3 * other + 2], x[3 * layer + 2])
            t = rate(pick) * s
            plane = added(plane, t)
            if abs(dz) == 1:
                lift = added(lift, t if dz > 0 else -t)
            if abs(dz) == 2:
                lift = added(lift, scaled(dz, t))
        if di or dj:
            plane = plane * here
            if di:
                total[3 * layer] = added(total[3 * layer], scaled(di, plane))
            if dj:
                total[3 * layer + 1] = added(total[3 * layer + 1], scaled(dj, plane))
        total[3 * layer + 2] = added(total[3 * layer + 2], lift * here)


def pair_kernel(adv, codes, flags, mask, force, base, strengths, rates, present, impact, turned, held, moved, far, spare):
    ply, stripe = place()
    cell, lane = lanes_and_cells()
    for side in range(2):
        rows = []
        for field in range(12):
            whole = adv[field % 3, 0, field // 3]
            rows.append(whole if side == 0 else pltpu.roll(whole, 4, 0))
        stacked = jnp.concatenate(rows, axis=0)
        for piece in range(4):
            turned[side, 128 * piece : 128 * piece + 128, 0:96] = stacked[:, 128 * piece : 128 * piece + 128].T
    for position in range(8):
        pick = pl.ds(position, TURNS, stride=8)
        both = jnp.concatenate([turned[0, pick, :], turned[1, pick, :]], axis=0)
        held[96 * position : 96 * position + 96] = both.T[0:96]
    for field in range(12):
        for q in range(8):
            value = held[pl.ds(8 * field + q, 8, stride=96), :]
            base[field, q] = value
            if q < 4:
                others, after, before = shifted_by(value, cell)
                for dj, other in others.items():
                    moved[dj + 2, field, q] = other
                if field % 3 == 1:
                    far[0, field // 3, q] = pltpu.roll(jnp.where(cell >= 5, before, value), 3, 0)
                    far[1, field // 3, q] = pltpu.roll(jnp.where(cell < 3, after, value), 5, 0)
    row = 8 * stripe + jnp.where(lane >= TURNS, 4, 0)
    column = 8 * jnp.bitwise_and(lane, TURNS - 1) + cell
    row_in = [(row + q >= 0) & (row + q < CELLS) for q in range(-3, 7)]
    for dj in range(-3, 4):
        column_in = (column + dj >= 0) & (column + dj < CELLS)
        for q in range(-3, 7):
            present[dj + 3, q + 3] = (row_in[q + 3] & column_in).astype(F32)
    spare[0:1, 0:TURNS] = flags[0, 0]
    spare[1:2, 0:TURNS] = flags[0, 1]
    both = spare[...]
    both = jnp.where(lane < TURNS, both, pltpu.roll(both, TURNS, 1))
    plain = [jnp.broadcast_to(both[word : word + 1], (8, 128)) for word in range(2)]
    top = ply == (lax.axis_size("ply") if not INTERPRET else 8) - 1
    lower = jnp.where(top, 0.0, 1.0)
    for spot, (di, dj) in enumerate(PLANE):
        for dz in (1, 2, 3):
            if dz * dz + di * di + dj * dj <= 9:
                k = class_index(dz, di, dj)
                whole = jnp.bitwise_and(plain[k // 30], 1 << (k % 30)) == 0
                strength = jnp.where(whole, lower * weight(dz, di, dj), 0.0)
                for m in range(4):
                    strengths[dz - 1 if dz < 3 else 0, spot if dz < 3 else 25, m] = strength * present[dj + 3, m + di + 3]
    impact[...] = (IMPACT * top.astype(F32)) * mask[...].astype(F32)
    cos_parts, sin_parts = [], []
    for side in range(2):
        code = codes[0, side]
        cosine = jnp.where(code == 0, 1.0, jnp.where(code == 1, 0.0, ROOT_HALF))
        sine = jnp.where(code == 0, 0.0, jnp.where(code == 1, 1.0, jnp.where(code == 2, ROOT_HALF, -ROOT_HALF)))
        cos_parts.append(jnp.full((8, 128), cosine, F32))
        sin_parts.append(jnp.full((8, 128), sine, F32))
    for spot, (di, dj) in enumerate(PLANE):
        lean = [(di * cos_parts[side] + dj * sin_parts[side]) ** 2 for side in range(2)]
        if (di, dj) != (0, 0):
            rates[spot, 0] = coefficient(lean[0], lean[0], 0, di, dj)
            rates[spot, 1] = coefficient(lean[1], lean[1], 0, di, dj)
        rates[spot, 2] = coefficient(lean[0], lean[0], 1, di, dj)
        rates[spot, 3] = coefficient(lean[0], lean[1], 1, di, dj)
        rates[spot, 4] = coefficient(lean[1], lean[1], 1, di, dj)
        rates[spot, 5] = coefficient(lean[0], lean[1], 2, di, dj)
    for side in range(2):
        lean = (3 * cos_parts[side]) ** 2
        rates[25, side] = 9.0 * coefficient(lean, lean, 0, 3, 0)
        lean = (3 * sin_parts[side]) ** 2
        rates[25, 2 + side] = 9.0 * coefficient(lean, lean, 0, 0, 3)
    rates[25, 4] = 9.0 * coefficient(jnp.zeros((8, 128), F32), 0.0, 3, 0, 0)
    for m in range(4):
        x = [base[field, m] for field in range(12)]
        rise = rates[25, 4] * (x[11] - x[2])
        total = [None] * 12
        total[2], total[11] = rise, -rise
        for spot, (di, dj) in enumerate(PLANE):
            q = m + di
            if 0 <= q < 4:
                y = [moved[dj + 2, field, q] if dj else base[field, q] for field in range(12)]
                pair_bonds(di, dj, x, y, present[dj + 3, q + 3], lambda pick: rates[spot, pick], total)
        for layer in range(4):
            for step in (-3, 3):
                if 0 <= m + step < 4:
                    apart = base[3 * layer, m + step] - x[3 * layer]
                    total[3 * layer] = added(total[3 * layer], rates[25, layer // 2] * apart)
            for side, step in ((0, -3), (1, 3)):
                apart = present[3 + step, m + 3] * (far[side, layer, m] - x[3 * layer + 1])
                total[3 * layer + 1] = total[3 * layer + 1] + rates[25, 2 + layer // 2] * apart
        for field in range(12):
            force[field, m] = total[field]


def weight(dz, di, dj):
    return INTER_C * RATE / float(dz * dz + di * di + dj * dj) ** 1.5


EDGE_ROWS = (-2, -1, 4, 5)


def edge_kernel(low, high, base, rates, present, partial, force, turned, held, moved):
    cell, lane = lanes_and_cells()
    left = lane < TURNS
    for side, rows in enumerate((low, high)):
        for piece in range(4):
            turned[side, 128 * piece : 128 * piece + 128, 0:40] = rows[:, 128 * piece : 128 * piece + 128].T
    for position in range(8):
        pick = pl.ds(position, TURNS, stride=8)
        both = jnp.concatenate([turned[0, pick, :], turned[1, pick, :]], axis=0)
        held[40 * position : 40 * position + 40] = both.T[0:40]

    def around(field, q):
        other = held[pl.ds(3 * field + (q + 3 if q < 0 else q - 4), 8, stride=40), :]
        return jnp.where(left, other, base[field, q + 8]) if q < 0 else jnp.where(left, base[field, q], other)

    for field in range(12):
        for spot, q in enumerate(EDGE_ROWS):
            value = around(field, q)
            moved[2, field, spot] = value
            for dj, other in shifted_by(value, cell)[0].items():
                moved[dj + 2, field, spot] = other
    for m in range(4):
        x = [base[field, m] for field in range(12)]
        total = [partial[field, m] for field in range(12)]
        for spot, (di, dj) in enumerate(PLANE):
            q = m + di
            if q in EDGE_ROWS:
                y = [moved[dj + 2, field, EDGE_ROWS.index(q)] for field in range(12)]
                pair_bonds(di, dj, x, y, present[dj + 3, q + 3], lambda pick: rates[spot, pick], total)
        for layer in range(4):
            for q in (m - 3, m + 3):
                if q < 0 or q > 3:
                    apart = present[3, q + 3] * (around(3 * layer, q) - x[3 * layer])
                    total[3 * layer] = total[3 * layer] + rates[25, layer // 2] * apart
        for field in range(12):
            force[field, m] = total[field]


def grown(sums, key, sign, value):
    if key not in sums:
        sums[key] = value if sign > 0 else -value
    else:
        sums[key] = sums[key] + value if sign > 0 else sums[key] - value


def stretched(turn, far, near, rise, far_z, near_z):
    lift = far_z - near_z
    if abs(rise) == 2:
        lift = lift + lift
    if far is None:
        return lift, 1 if rise > 0 else -1
    core = far - near
    if rise > 0:
        return (core + lift if turn > 0 else lift - core), 1
    return (core - lift, 1) if turn > 0 else (core + lift, -1)


def pushed(sums, wide, field, di, dj, sign, value):
    for step, spot in ((di, field), (dj, field + 1)):
        if step:
            grown(sums if abs(step) == 1 else wide, spot, sign if step > 0 else -sign, value)


def interface_kernel(message, own, strengths, force, half, impact, new_v, new_a, facing, moved, below, shared, turned):
    ply, stripe = place()
    cell, lane = lanes_and_cells()
    wide_lane = lax.broadcasted_iota(I32, (TURNS, 128), 1)
    lines = [message[pl.ds(row, TURNS, stride=WINDOW), :] for row in range(WINDOW)]
    last = lines[0]
    for row, start in SPREAD:
        last = jnp.where(wide_lane < start, last, pltpu.roll(lines[row], start + 16, 1))
    lines.append(last)
    for q in range(8):
        facing[q] = jnp.concatenate([lines[q], lines[q + 4]], axis=0).T
    row = 8 * stripe + jnp.where(lane >= TURNS, 4, 0)
    column = 8 * jnp.bitwise_and(lane, TURNS - 1) + cell
    left = lane < TURNS
    same = facing[4, 112:120]
    twin = pltpu.roll(same, TURNS, 1)
    for parts, spots in (
        (jnp.where(left, facing[0, 112:120], same), (0, 1)),
        (jnp.where(left, twin, same), (2, 3, 4, 5)),
        (jnp.where(left, twin, facing[6, 112:120]), (6, 7)),
    ):
        parts = parts.astype(I32)
        joined = [jnp.bitwise_or(jnp.left_shift(parts[1:2], 15), parts[0:1]), parts[2:3]]
        for word in range(2):
            plain = jnp.broadcast_to(joined[word], (8, 128))
            before, after = pltpu.roll(plain, 1, 1), pltpu.roll(plain, 127, 1)
            for dj in range(-2, 3):
                turned_word = plain
                if dj < 0:
                    turned_word = jnp.where(cell + dj < 0, before, plain)
                if dj > 0:
                    turned_word = jnp.where(cell + dj > 7, after, plain)
                column_in = (column + dj >= 0) & (column + dj < CELLS) & (ply > 0)
                for q in spots:
                    good = (row + q - 2 >= 0) & (row + q - 2 < CELLS) & column_in
                    below[word, dj + 2, q] = jnp.where(good, turned_word, -1)

    def spread(q):
        for slot in (0, 1, 2, 3, 4, 5, 7, 8, 9, 10, 11, 12):
            field = facing[q, 8 * slot : 8 * slot + 8]
            moved[slot, q, 0:8] = pltpu.roll(field, 1, 1)
            moved[slot, q, 8:16] = field
            moved[slot, q, 16:24] = pltpu.roll(field, 127, 1)

    def kept(dz, di, dj, spot):
        k = class_index(dz, -dj, -di)
        whole = jnp.bitwise_and(below[k // 30, dj + 2, spot], 1 << (k % 30)) == 0
        return jnp.where(whole, weight(dz, di, dj), 0.0)

    def bonds(m):
        x = [own[field, m] for field in range(12)]
        sums = {field: force[field, m] for field in range(12)}
        wide, double = {}, {}
        for spot, (di, dj) in enumerate(PLANE):
            q = m + 2 + di
            close = di * di + dj * dj <= 5
            turn = 1 if (di, dj) >= (0, 0) else -1
            pi, pj = turn * di, turn * dj

            def y(slot):
                return moved[slot, q, 8 + dj : 16 + dj]

            far, far_z = along(pi, pj, y(0), y(1)), y(2)
            near = along(pi, pj, x[9], x[10])
            value, sign = stretched(turn, far, near, 1, far_z, x[11])
            first = strengths[0, spot, m] * value
            grown(sums, 11, sign, first)
            plane = first
            if close:
                value, sign = stretched(turn, along(pi, pj, y(3), y(4)), near, 2, y(5), x[11])
                second = strengths[1, spot, m] * value
                grown(double, 11, sign, second)
                plane = first + second
                value, sign = stretched(turn, far, along(pi, pj, x[6], x[7]), 2, far_z, x[8])
                second = strengths[1, spot, m] * value
                grown(double, 8, sign, second)
                pushed(sums, wide, 6, di, dj, sign, second)
            pushed(sums, wide, 9, di, dj, sign, plane)
            far, far_z = along(pi, pj, y(7), y(8)), y(9)
            near = along(pi, pj, x[0], x[1])
            value, sign = stretched(turn, far, near, -1, far_z, x[2])
            first = kept(1, di, dj, q) * value
            grown(sums, 2, -sign, first)
            plane = first
            if close:
                value, sign = stretched(turn, along(pi, pj, y(10), y(11)), near, -2, y(12), x[2])
                strength = kept(2, di, dj, q)
                second = strength * value
                grown(double, 2, -sign, second)
                plane = first + second
                value, sign = stretched(turn, far, along(pi, pj, x[3], x[4]), -2, far_z, x[5])
                second = strength * value
                grown(double, 5, -sign, second)
                pushed(sums, wide, 3, di, dj, sign, second)
            pushed(sums, wide, 0, di, dj, sign, plane)
            if di == 0 and dj == 0:
                rise = 9.0 * strengths[0, 25, m]
                grown(sums, 11, 1, rise * (facing[q, 48:56] - x[11]))
                grown(sums, 8, 1, rise * (y(5) - x[8]))
                grown(sums, 5, 1, rise * (y(2) - x[5]))
                rise = 9.0 * kept(3, 0, 0, q)
                grown(sums, 2, 1, rise * (facing[q, 104:112] - x[2]))
                grown(sums, 5, 1, rise * (y(12) - x[5]))
                grown(sums, 8, 1, rise * (y(9) - x[8]))
        for extra in (wide, double):
            for field, value in extra.items():
                sums[field] = sums[field] + 2.0 * value
        for field in range(12):
            shared[8 * field + m] = sums[field]
            shared[8 * field + 4 + m] = sums[field]

    for q in range(4):
        spread(q)
    for m in range(4):
        spread(m + 4)
        bonds(m)
    flat = shared.reshape(96 * 8, 128)
    low_row = jnp.bitwise_and(lax.broadcasted_iota(I32, (TURNS, 96), 1), 7) < 4
    for position in range(8):
        both = flat[pl.ds(position, 96, stride=8), :].T
        turned[pl.ds(position, TURNS, stride=8), 0:96] = jnp.where(low_row, both[0:TURNS], both[TURNS:])
    for piece in range(4):
        columns = slice(128 * piece, 128 * piece + 128)
        back = turned[columns, :].T
        for layer in range(4):
            for comp in range(3):
                field = 3 * layer + comp
                value = back[8 * field : 8 * field + 8]
                if field == 11:
                    value = value - impact[:, columns]
                new_a[comp, 0, layer, :, columns] = value
                new_v[comp, 0, layer, :, columns] = half[comp, 0, layer, :, columns] + 0.5 * value


def shape(*dims, dtype=F32):
    return jax.ShapeDtypeStruct(dims, dtype)


def near(*dims, dtype=F32):
    return shape(*dims, dtype=dtype) if INTERPRET else pltpu.VMEM(dims, dtype)


def kept_near(array):
    return array if INTERPRET else pltpu.with_memory_space_constraint(array, pltpu.VMEM)


def run_advance(displacement, velocity, acceleration, flags):
    return pl.pallas_call(
        advance_kernel,
        out_shape=(
            near(3, 1, 4, ROWS, CELLS),
            near(3, 1, 4, ROWS, CELLS),
            near(64, CELLS),
            near(64, CELLS),
            near(40, CELLS),
            near(40, CELLS),
        ),
        interpret=INTERPRET,
    )(displacement, velocity, acceleration, flags)


def run_turn(one, two):
    return pl.pallas_call(
        turn_kernel,
        out_shape=near(TURNS * WINDOW, 128),
        scratch_shapes=[pltpu.VMEM((CELLS + 16, 128), F32)],
        interpret=INTERPRET,
        compiler_params=pltpu.CompilerParams(vmem_limit_bytes=16 * 1024 * 1024),
    )(kept_near(one), kept_near(two))


def run_pair(adv, codes, flags, mask):
    vmem = pl.BlockSpec(memory_space=pltpu.VMEM)
    return pl.pallas_call(
        pair_kernel,
        out_shape=(
            near(12, 4, 8, 128),
            near(12, 8, 8, 128),
            near(2, 26, 4, 8, 128),
            near(26, 6, 8, 128),
            near(7, 10, 8, 128),
            near(8, CELLS),
        ),
        in_specs=[vmem, pl.BlockSpec(memory_space=pltpu.SMEM), vmem, vmem],
        scratch_shapes=[
            pltpu.VMEM((2, CELLS, 128), F32),
            pltpu.VMEM((8 * 96, 128), F32),
            pltpu.VMEM((5, 12, 4, 8, 128), F32),
            pltpu.VMEM((2, 4, 4, 8, 128), F32),
            pltpu.VMEM((8, 128), I32),
        ],
        interpret=INTERPRET,
        compiler_params=pltpu.CompilerParams(vmem_limit_bytes=16 * 1024 * 1024),
        cost_estimate=pl.CostEstimate(flops=20_000_000, bytes_accessed=1_000_000, transcendentals=0),
    )(kept_near(adv), codes, flags, mask)


def run_edge(low, high, base, rates, present, partial):
    return pl.pallas_call(
        edge_kernel,
        out_shape=near(12, 4, 8, 128),
        scratch_shapes=[
            pltpu.VMEM((2, CELLS, 128), F32),
            pltpu.VMEM((8 * 40, 128), F32),
            pltpu.VMEM((5, 12, 4, 8, 128), F32),
        ],
        interpret=INTERPRET,
        compiler_params=pltpu.CompilerParams(vmem_limit_bytes=16 * 1024 * 1024),
        cost_estimate=pl.CostEstimate(flops=10_000_000, bytes_accessed=1_000_000, transcendentals=0),
    )(*[kept_near(array) for array in (low, high, base, rates, present, partial)])


def run_interface(message, own, strengths, force, half, impact):
    return pl.pallas_call(
        interface_kernel,
        out_shape=(shape(3, 1, 4, ROWS, CELLS), shape(3, 1, 4, ROWS, CELLS)),
        scratch_shapes=[
            pltpu.VMEM((8, 128, 128), F32),
            pltpu.VMEM((13, 8, 24, 128), F32),
            pltpu.VMEM((2, 5, 8, 8, 128), I32),
            pltpu.VMEM((96, 8, 128), F32),
            pltpu.VMEM((CELLS, 128), F32),
        ],
        interpret=INTERPRET,
        compiler_params=pltpu.CompilerParams(vmem_limit_bytes=16 * 1024 * 1024),
    )(kept_near(message), kept_near(own), kept_near(strengths), kept_near(force), kept_near(half), kept_near(impact))


def steps(axis, by):
    count = lax.axis_size(axis)
    return [(i, i + by) for i in range(count) if 0 <= i + by < count]


def swaps(axis, start):
    count = lax.axis_size(axis)
    pairs = [(i, i + 1) for i in range(start, count - 1, 2)]
    return pairs + [(j, i) for i, j in pairs]


def local(displacement, velocity, acceleration, fibre_codes, contact_mask, bond_flags):
    adv, half, one, two, low, high = run_advance(displacement, velocity, acceleration, bond_flags)
    one = lax.ppermute(one, "ply", swaps("ply", 0))
    two = lax.ppermute(two, "ply", swaps("ply", 1))
    low = lax.ppermute(low, "stripe", steps("stripe", 1))
    high = lax.ppermute(high, "stripe", steps("stripe", -1))
    message = run_turn(one, two).reshape(TURNS, 1, WINDOW * 128)
    message = lax.all_to_all(message, "stripe", 0, 0)
    partial, own, strengths, rates, present, impact = run_pair(adv, fibre_codes, bond_flags, contact_mask)
    force = run_edge(low, high, own, rates, present, partial)
    message = message.reshape(TURNS * WINDOW, 128)
    new_velocity, new_acceleration = run_interface(message, own, strengths, force, half, impact)
    return adv, new_velocity, new_acceleration


def solution(mesh):
    state = P(None, "ply", None, "stripe", None)
    return jax.shard_map(
        local,
        mesh=mesh,
        in_specs=(state, state, state, P("ply", None), P("stripe", None), P("ply", None, "stripe", None)),
        out_specs=(state, state, state),
        check_vma=False,
    )
```

```python
import jax
import jax.numpy as jnp
from jax import lax
from jax.experimental import pallas as pl
from jax.experimental.pallas import tpu as pltpu
from jax.sharding import PartitionSpec as P


ROOT_HALF = 0.7071067811865476
RATE = 0.025
MATRIX_C = 1.0
FIBRE_C = 4.0
INTER_C = 1.5
IMPACT = 2.0

F32 = jnp.float32
I32 = jnp.int32
ROWS = 8
TURNS = 64
CELLS = ROWS * TURNS
WINDOW = 11
SPREAD = [(2, 0), (3, 16), (4, 32), (5, 56), (6, 72), (7, 88)]
PLANE = [(di, dj) for di in range(-2, 3) for dj in range(-2, 3)]
INTERPRET = False


def place():
    return lax.axis_index("ply"), lax.axis_index("stripe")


def class_index(dz, di, dj):
    count = 0
    for z in range(1, 4):
        for i in range(-3, 4):
            for j in range(-3, 4):
                if z * z + i * i + j * j <= 9:
                    if (z, i, j) == (dz, di, dj):
                        return count
                    count += 1
    raise ValueError("no class")


def scaled(factor, value):
    if factor == 1:
        return value
    if factor == -1:
        return -value
    return factor * value


def along(di, dj, first, second):
    if di == 0 and dj == 0:
        return None
    if di == 0:
        return scaled(dj, second)
    if dj == 0:
        return scaled(di, first)
    if abs(di) == abs(dj):
        inner = first + second if di == dj else first - second
        return scaled(di, inner)
    return scaled(di, first) + scaled(dj, second)


def gap(far, near, rise, far_z, near_z):
    total = None if far is None else far - near
    if rise:
        lift = scaled(rise, far_z - near_z)
        total = lift if total is None else total + lift
    return total


def added(total, value):
    return value if total is None else total + value


def lanes_and_cells():
    cell = lax.broadcasted_iota(I32, (8, 128), 0)
    lane = lax.broadcasted_iota(I32, (8, 128), 1)
    return cell, lane


def shifted_by(value, cell):
    after = pltpu.roll(value, 127, 1)
    before = pltpu.roll(value, 1, 1)
    moved = {}
    for dj in (1, 2):
        moved[dj] = pltpu.roll(jnp.where(cell < dj, after, value), 8 - dj, 0)
        moved[-dj] = pltpu.roll(jnp.where(cell >= 8 - dj, before, value), dj, 0)
    return moved, after, before


def advance_kernel(disp, vel, acc, flags, adv, half, one, two, low, high):
    values = []
    for layer in range(4):
        for comp in range(3):
            speed = vel[comp, 0, layer] + 0.5 * acc[comp, 0, layer]
            moved = disp[comp, 0, layer] + speed
            half[comp, 0, layer] = speed
            adv[comp, 0, layer] = moved
            count = 2 if comp else 3
            start = 7 * layer + (0, 3, 5)[comp]
            low[start : start + count] = moved[8 - count : 8]
            high[start : start + count] = moved[0:count]
            values.append(moved)
    low[28:32] = jnp.zeros((4, CELLS), F32)
    high[28:32] = jnp.zeros((4, CELLS), F32)
    even = jnp.bitwise_and(place()[0], 1) == 0
    for slot, fields in enumerate(zip((1, 0, 2, 4, 3, 5, 8), (10, 9, 11, 7, 6, 8, 5))):
        to_lower, to_upper = (values[field] for field in fields)
        one[8 * slot : 8 * slot + 8] = jnp.where(even, to_upper, to_lower)
        two[8 * slot : 8 * slot + 8] = jnp.where(even, to_lower, to_upper)
    first = flags[0, 0]
    second = flags[0, 1]
    parts = jnp.concatenate(
        [jnp.bitwise_and(first, 0x7FFF), jnp.right_shift(first, 15), second, jnp.zeros((5, TURNS), I32)],
        axis=0,
    ).astype(F32)
    block = lax.broadcasted_iota(I32, (TURNS, CELLS), 0)
    column = lax.broadcasted_iota(I32, (TURNS, CELLS), 1)
    spread = (jnp.right_shift(column, 3) == block).astype(F32)
    spread_parts = jnp.dot(parts, spread, precision=lax.Precision.HIGHEST, preferred_element_type=F32)
    one[56:64] = spread_parts
    two[56:64] = spread_parts


def turn_kernel(one, two, message, turned):
    even = jnp.bitwise_and(place()[0], 1) == 0
    first, second = one[...], two[...]
    above = jnp.where(even, first[0:56], second[0:56])
    below = jnp.where(even, second, first)
    stacked = jnp.concatenate([above, below, jnp.zeros((8, CELLS), F32)], axis=0)
    turned[0:8] = jnp.zeros((8, 128), F32)
    turned[CELLS + 8 : CELLS + 16] = jnp.zeros((8, 128), F32)
    for piece in range(4):
        turned[8 + 128 * piece : 136 + 128 * piece] = stacked[:, 128 * piece : 128 * piece + 128].T
    lane = lax.broadcasted_iota(I32, (TURNS, 128), 1)
    last = turned[pl.ds(17, TURNS, stride=8), :]
    starts = dict(SPREAD)
    for row in range(WINDOW):
        line = turned[pl.ds(6 + row, TURNS, stride=8), :]
        if row in starts:
            line = jnp.where(lane < 112, line, pltpu.roll(last, 112 - starts[row], 1))
        message[pl.ds(row, TURNS, stride=WINDOW), :] = line


def coefficient(here, there, dz, di, dj):
    radius = float(dz * dz + di * di + dj * dj)
    level = RATE / radius**1.5
    return level * MATRIX_C + (level * FIBRE_C * 0.5 / radius) * (here + there)


def pair_bonds(di, dj, x, y, here, rate, total):
    far_e = [along(di, dj, y[3 * l], y[3 * l + 1]) for l in range(4)]
    near_e = [along(di, dj, x[3 * l], x[3 * l + 1]) for l in range(4)]
    for layer in range(4):
        plane, lift = None, None
        for other in range(4):
            dz = other - layer
            if dz * dz + di * di + dj * dj > 9 or (dz, di, dj) == (0, 0, 0) or abs(dz) == 3:
                continue
            pick = (layer // 2, 2 + min(layer, other), 5)[abs(dz)]
            s = gap(far_e[other], near_e[layer], dz, y[3 * other + 2], x[3 * layer + 2])
            t = rate(pick) * s
            plane = added(plane, t)
            if abs(dz) == 1:
                lift = added(lift, t if dz > 0 else -t)
            if abs(dz) == 2:
                lift = added(lift, scaled(dz, t))
        if di or dj:
            plane = plane * here
            if di:
                total[3 * layer] = added(total[3 * layer], scaled(di, plane))
            if dj:
                total[3 * layer + 1] = added(total[3 * layer + 1], scaled(dj, plane))
        total[3 * layer + 2] = added(total[3 * layer + 2], lift * here)


def pair_kernel(adv, codes, flags, mask, force, base, strengths, rates, present, impact, turned, held, moved, far, spare):
    ply, stripe = place()
    cell, lane = lanes_and_cells()
    for side in range(2):
        rows = []
        for field in range(12):
            whole = adv[field % 3, 0, field // 3]
            rows.append(whole if side == 0 else pltpu.roll(whole, 4, 0))
        stacked = jnp.concatenate(rows, axis=0)
        for piece in range(4):
            turned[side, 128 * piece : 128 * piece + 128, 0:96] = stacked[:, 128 * piece : 128 * piece + 128].T
    for position in range(8):
        pick = pl.ds(position, TURNS, stride=8)
        both = jnp.concatenate([turned[0, pick, :], turned[1, pick, :]], axis=0)
        held[96 * position : 96 * position + 96] = both.T[0:96]
    for field in range(12):
        for q in range(8):
            value = held[pl.ds(8 * field + q, 8, stride=96), :]
            base[field, q] = value
            if q < 4:
                others, after, before = shifted_by(value, cell)
                for dj, other in others.items():
                    moved[dj + 2, field, q] = other
                if field % 3 == 1:
                    far[0, field // 3, q] = pltpu.roll(jnp.where(cell >= 5, before, value), 3, 0)
                    far[1, field // 3, q] = pltpu.roll(jnp.where(cell < 3, after, value), 5, 0)
    row = 8 * stripe + jnp.where(lane >= TURNS, 4, 0)
    column = 8 * jnp.bitwise_and(lane, TURNS - 1) + cell
    row_in = [(row + q >= 0) & (row + q < CELLS) for q in range(-3, 7)]
    for dj in range(-3, 4):
        column_in = (column + dj >= 0) & (column + dj < CELLS)
        for q in range(-3, 7):
            present[dj + 3, q + 3] = (row_in[q + 3] & column_in).astype(F32)
    spare[0:1, 0:TURNS] = flags[0, 0]
    spare[1:2, 0:TURNS] = flags[0, 1]
    both = spare[...]
    both = jnp.where(lane < TURNS, both, pltpu.roll(both, TURNS, 1))
    plain = [jnp.broadcast_to(both[word : word + 1], (8, 128)) for word in range(2)]
    top = ply == (lax.axis_size("ply") if not INTERPRET else 8) - 1
    lower = jnp.where(top, 0.0, 1.0)
    for spot, (di, dj) in enumerate(PLANE):
        for dz in (1, 2, 3):
            if dz * dz + di * di + dj * dj <= 9:
                k = class_index(dz, di, dj)
                whole = jnp.bitwise_and(plain[k // 30], 1 << (k % 30)) == 0
                strength = jnp.where(whole, lower * weight(dz, di, dj), 0.0)
                for m in range(4):
                    strengths[dz - 1 if dz < 3 else 0, spot if dz < 3 else 25, m] = strength * present[dj + 3, m + di + 3]
    impact[...] = (IMPACT * top.astype(F32)) * mask[...].astype(F32)
    cos_parts, sin_parts = [], []
    for side in range(2):
        code = codes[0, side]
        cosine = jnp.where(code == 0, 1.0, jnp.where(code == 1, 0.0, ROOT_HALF))
        sine = jnp.where(code == 0, 0.0, jnp.where(code == 1, 1.0, jnp.where(code == 2, ROOT_HALF, -ROOT_HALF)))
        cos_parts.append(jnp.full((8, 128), cosine, F32))
        sin_parts.append(jnp.full((8, 128), sine, F32))
    for spot, (di, dj) in enumerate(PLANE):
        lean = [(di * cos_parts[side] + dj * sin_parts[side]) ** 2 for side in range(2)]
        if (di, dj) != (0, 0):
            rates[spot, 0] = coefficient(lean[0], lean[0], 0, di, dj)
            rates[spot, 1] = coefficient(lean[1], lean[1], 0, di, dj)
        rates[spot, 2] = coefficient(lean[0], lean[0], 1, di, dj)
        rates[spot, 3] = coefficient(lean[0], lean[1], 1, di, dj)
        rates[spot, 4] = coefficient(lean[1], lean[1], 1, di, dj)
        rates[spot, 5] = coefficient(lean[0], lean[1], 2, di, dj)
    for side in range(2):
        lean = (3 * cos_parts[side]) ** 2
        rates[25, side] = 9.0 * coefficient(lean, lean, 0, 3, 0)
        lean = (3 * sin_parts[side]) ** 2
        rates[25, 2 + side] = 9.0 * coefficient(lean, lean, 0, 0, 3)
    rates[25, 4] = 9.0 * coefficient(jnp.zeros((8, 128), F32), 0.0, 3, 0, 0)
    for m in range(4):
        x = [base[field, m] for field in range(12)]
        rise = rates[25, 4] * (x[11] - x[2])
        total = [None] * 12
        total[2], total[11] = rise, -rise
        for spot, (di, dj) in enumerate(PLANE):
            q = m + di
            if 0 <= q < 4:
                y = [moved[dj + 2, field, q] if dj else base[field, q] for field in range(12)]
                pair_bonds(di, dj, x, y, present[dj + 3, q + 3], lambda pick: rates[spot, pick], total)
        for layer in range(4):
            for step in (-3, 3):
                if 0 <= m + step < 4:
                    apart = base[3 * layer, m + step] - x[3 * layer]
                    total[3 * layer] = added(total[3 * layer], rates[25, layer // 2] * apart)
            for side, step in ((0, -3), (1, 3)):
                apart = present[3 + step, m + 3] * (far[side, layer, m] - x[3 * layer + 1])
                total[3 * layer + 1] = total[3 * layer + 1] + rates[25, 2 + layer // 2] * apart
        for field in range(12):
            force[field, m] = total[field]


def weight(dz, di, dj):
    return INTER_C * RATE / float(dz * dz + di * di + dj * dj) ** 1.5


EDGE_ROWS = (-2, -1, 4, 5)


def edge_kernel(low, high, base, rates, present, partial, force, turned, held, moved):
    cell, lane = lanes_and_cells()
    left = lane < TURNS
    for side, rows in enumerate((low, high)):
        for piece in range(4):
            turned[side, 128 * piece : 128 * piece + 128, 0:32] = rows[:, 128 * piece : 128 * piece + 128].T
    for position in range(8):
        pick = pl.ds(position, TURNS, stride=8)
        both = jnp.concatenate([turned[0, pick, :], turned[1, pick, :]], axis=0)
        held[32 * position : 32 * position + 32] = both.T[0:32]

    def around(field, q):
        layer, comp = field // 3, field % 3
        count = 2 if comp else 3
        start = 7 * layer + (0, 3, 5)[comp]
        other = held[pl.ds(start + (q + count if q < 0 else q - 4), 8, stride=32), :]
        return jnp.where(left, other, base[field, q + 8]) if q < 0 else jnp.where(left, base[field, q], other)

    for field in range(12):
        for spot, q in enumerate(EDGE_ROWS):
            value = around(field, q)
            moved[2, field, spot] = value
            for dj, other in shifted_by(value, cell)[0].items():
                moved[dj + 2, field, spot] = other
    for m in range(4):
        x = [base[field, m] for field in range(12)]
        total = [partial[field, m] for field in range(12)]
        for spot, (di, dj) in enumerate(PLANE):
            q = m + di
            if q in EDGE_ROWS:
                y = [moved[dj + 2, field, EDGE_ROWS.index(q)] for field in range(12)]
                pair_bonds(di, dj, x, y, present[dj + 3, q + 3], lambda pick: rates[spot, pick], total)
        for layer in range(4):
            for q in (m - 3, m + 3):
                if q < 0 or q > 3:
                    apart = present[3, q + 3] * (around(3 * layer, q) - x[3 * layer])
                    total[3 * layer] = total[3 * layer] + rates[25, layer // 2] * apart
        for field in range(12):
            force[field, m] = total[field]


def grown(sums, key, sign, value):
    if key not in sums:
        sums[key] = value if sign > 0 else -value
    else:
        sums[key] = sums[key] + value if sign > 0 else sums[key] - value


def stretched(turn, far, near, rise, far_z, near_z):
    lift = far_z - near_z
    if abs(rise) == 2:
        lift = lift + lift
    if far is None:
        return lift, 1 if rise > 0 else -1
    core = far - near
    if rise > 0:
        return (core + lift if turn > 0 else lift - core), 1
    return (core - lift, 1) if turn > 0 else (core + lift, -1)


def pushed(sums, wide, field, di, dj, sign, value):
    for step, spot in ((di, field), (dj, field + 1)):
        if step:
            grown(sums if abs(step) == 1 else wide, spot, sign if step > 0 else -sign, value)


def interface_kernel(message, own, strengths, force, half, impact, new_v, new_a, facing, moved, below, shared, turned):
    ply, stripe = place()
    cell, lane = lanes_and_cells()
    wide_lane = lax.broadcasted_iota(I32, (TURNS, 128), 1)
    lines = [message[pl.ds(row, TURNS, stride=WINDOW), :] for row in range(WINDOW)]
    last = lines[0]
    for row, start in SPREAD:
        last = jnp.where(wide_lane < start, last, pltpu.roll(lines[row], start + 16, 1))
    lines.append(last)
    for q in range(8):
        facing[q] = jnp.concatenate([lines[q], lines[q + 4]], axis=0).T
    row = 8 * stripe + jnp.where(lane >= TURNS, 4, 0)
    column = 8 * jnp.bitwise_and(lane, TURNS - 1) + cell
    left = lane < TURNS
    same = facing[4, 112:120]
    twin = pltpu.roll(same, TURNS, 1)
    for parts, spots in (
        (jnp.where(left, facing[0, 112:120], same), (0, 1)),
        (jnp.where(left, twin, same), (2, 3, 4, 5)),
        (jnp.where(left, twin, facing[6, 112:120]), (6, 7)),
    ):
        parts = parts.astype(I32)
        joined = [jnp.bitwise_or(jnp.left_shift(parts[1:2], 15), parts[0:1]), parts[2:3]]
        for word in range(2):
            plain = jnp.broadcast_to(joined[word], (8, 128))
            before, after = pltpu.roll(plain, 1, 1), pltpu.roll(plain, 127, 1)
            for dj in range(-2, 3):
                turned_word = plain
                if dj < 0:
                    turned_word = jnp.where(cell + dj < 0, before, plain)
                if dj > 0:
                    turned_word = jnp.where(cell + dj > 7, after, plain)
                column_in = (column + dj >= 0) & (column + dj < CELLS) & (ply > 0)
                for q in spots:
                    good = (row + q - 2 >= 0) & (row + q - 2 < CELLS) & column_in
                    below[word, dj + 2, q] = jnp.where(good, turned_word, -1)

    def spread(q):
        for slot in (0, 1, 2, 3, 4, 5, 7, 8, 9, 10, 11, 12):
            field = facing[q, 8 * slot : 8 * slot + 8]
            moved[slot, q, 0:8] = pltpu.roll(field, 1, 1)
            moved[slot, q, 8:16] = field
            moved[slot, q, 16:24] = pltpu.roll(field, 127, 1)

    def kept(dz, di, dj, spot):
        k = class_index(dz, -dj, -di)
        whole = jnp.bitwise_and(below[k // 30, dj + 2, spot], 1 << (k % 30)) == 0
        return jnp.where(whole, weight(dz, di, dj), 0.0)

    def bonds(m):
        x = [own[field, m] for field in range(12)]
        sums = {field: force[field, m] for field in range(12)}
        wide, double = {}, {}
        for spot, (di, dj) in enumerate(PLANE):
            q = m + 2 + di
            close = di * di + dj * dj <= 5
            turn = 1 if (di, dj) >= (0, 0) else -1
            pi, pj = turn * di, turn * dj

            def y(slot):
                return moved[slot, q, 8 + dj : 16 + dj]

            far, far_z = along(pi, pj, y(0), y(1)), y(2)
            near = along(pi, pj, x[9], x[10])
            value, sign = stretched(turn, far, near, 1, far_z, x[11])
            first = strengths[0, spot, m] * value
            grown(sums, 11, sign, first)
            plane = first
            if close:
                value, sign = stretched(turn, along(pi, pj, y(3), y(4)), near, 2, y(5), x[11])
                second = strengths[1, spot, m] * value
                grown(double, 11, sign, second)
                plane = first + second
                value, sign = stretched(turn, far, along(pi, pj, x[6], x[7]), 2, far_z, x[8])
                second = strengths[1, spot, m] * value
                grown(double, 8, sign, second)
                pushed(sums, wide, 6, di, dj, sign, second)
            pushed(sums, wide, 9, di, dj, sign, plane)
            far, far_z = along(pi, pj, y(7), y(8)), y(9)
            near = along(pi, pj, x[0], x[1])
            value, sign = stretched(turn, far, near, -1, far_z, x[2])
            first = kept(1, di, dj, q) * value
            grown(sums, 2, -sign, first)
            plane = first
            if close:
                value, sign = stretched(turn, along(pi, pj, y(10), y(11)), near, -2, y(12), x[2])
                strength = kept(2, di, dj, q)
                second = strength * value
                grown(double, 2, -sign, second)
                plane = first + second
                value, sign = stretched(turn, far, along(pi, pj, x[3], x[4]), -2, far_z, x[5])
                second = strength * value
                grown(double, 5, -sign, second)
                pushed(sums, wide, 3, di, dj, sign, second)
            pushed(sums, wide, 0, di, dj, sign, plane)
            if di == 0 and dj == 0:
                rise = 9.0 * strengths[0, 25, m]
                grown(sums, 11, 1, rise * (facing[q, 48:56] - x[11]))
                grown(sums, 8, 1, rise * (y(5) - x[8]))
                grown(sums, 5, 1, rise * (y(2) - x[5]))
                rise = 9.0 * kept(3, 0, 0, q)
                grown(sums, 2, 1, rise * (facing[q, 104:112] - x[2]))
                grown(sums, 5, 1, rise * (y(12) - x[5]))
                grown(sums, 8, 1, rise * (y(9) - x[8]))
        for extra in (wide, double):
            for field, value in extra.items():
                sums[field] = sums[field] + 2.0 * value
        for field in range(12):
            shared[8 * field + m] = sums[field]
            shared[8 * field + 4 + m] = sums[field]

    for q in range(4):
        spread(q)
    for m in range(4):
        spread(m + 4)
        bonds(m)
    flat = shared.reshape(96 * 8, 128)
    low_row = jnp.bitwise_and(lax.broadcasted_iota(I32, (TURNS, 96), 1), 7) < 4
    for position in range(8):
        both = flat[pl.ds(position, 96, stride=8), :].T
        turned[pl.ds(position, TURNS, stride=8), 0:96] = jnp.where(low_row, both[0:TURNS], both[TURNS:])
    for piece in range(4):
        columns = slice(128 * piece, 128 * piece + 128)
        back = turned[columns, :].T
        for layer in range(4):
            for comp in range(3):
                field = 3 * layer + comp
                value = back[8 * field : 8 * field + 8]
                if field == 11:
                    value = value - impact[:, columns]
                new_a[comp, 0, layer, :, columns] = value
                new_v[comp, 0, layer, :, columns] = half[comp, 0, layer, :, columns] + 0.5 * value


def shape(*dims, dtype=F32):
    return jax.ShapeDtypeStruct(dims, dtype)


def near(*dims, dtype=F32):
    return shape(*dims, dtype=dtype) if INTERPRET else pltpu.VMEM(dims, dtype)


def kept_near(array):
    return array if INTERPRET else pltpu.with_memory_space_constraint(array, pltpu.VMEM)


def run_advance(displacement, velocity, acceleration, flags):
    return pl.pallas_call(
        advance_kernel,
        out_shape=(
            near(3, 1, 4, ROWS, CELLS),
            near(3, 1, 4, ROWS, CELLS),
            near(64, CELLS),
            near(64, CELLS),
            near(32, CELLS),
            near(32, CELLS),
        ),
        interpret=INTERPRET,
    )(displacement, velocity, acceleration, flags)


def run_turn(one, two):
    return pl.pallas_call(
        turn_kernel,
        out_shape=near(TURNS * WINDOW, 128),
        scratch_shapes=[pltpu.VMEM((CELLS + 16, 128), F32)],
        interpret=INTERPRET,
        compiler_params=pltpu.CompilerParams(vmem_limit_bytes=16 * 1024 * 1024),
    )(kept_near(one), kept_near(two))


def run_pair(adv, codes, flags, mask):
    vmem = pl.BlockSpec(memory_space=pltpu.VMEM)
    return pl.pallas_call(
        pair_kernel,
        out_shape=(
            near(12, 4, 8, 128),
            near(12, 8, 8, 128),
            near(2, 26, 4, 8, 128),
            near(26, 6, 8, 128),
            near(7, 10, 8, 128),
            near(8, CELLS),
        ),
        in_specs=[vmem, pl.BlockSpec(memory_space=pltpu.SMEM), vmem, vmem],
        scratch_shapes=[
            pltpu.VMEM((2, CELLS, 128), F32),
            pltpu.VMEM((8 * 96, 128), F32),
            pltpu.VMEM((5, 12, 4, 8, 128), F32),
            pltpu.VMEM((2, 4, 4, 8, 128), F32),
            pltpu.VMEM((8, 128), I32),
        ],
        interpret=INTERPRET,
        compiler_params=pltpu.CompilerParams(vmem_limit_bytes=16 * 1024 * 1024),
        cost_estimate=pl.CostEstimate(flops=20_000_000, bytes_accessed=1_000_000, transcendentals=0),
    )(kept_near(adv), codes, flags, mask)


def run_edge(low, high, base, rates, present, partial):
    return pl.pallas_call(
        edge_kernel,
        out_shape=near(12, 4, 8, 128),
        scratch_shapes=[
            pltpu.VMEM((2, CELLS, 128), F32),
            pltpu.VMEM((8 * 32, 128), F32),
            pltpu.VMEM((5, 12, 4, 8, 128), F32),
        ],
        interpret=INTERPRET,
        compiler_params=pltpu.CompilerParams(vmem_limit_bytes=16 * 1024 * 1024),
        cost_estimate=pl.CostEstimate(flops=10_000_000, bytes_accessed=1_000_000, transcendentals=0),
    )(*[kept_near(array) for array in (low, high, base, rates, present, partial)])


def run_interface(message, own, strengths, force, half, impact):
    return pl.pallas_call(
        interface_kernel,
        out_shape=(shape(3, 1, 4, ROWS, CELLS), shape(3, 1, 4, ROWS, CELLS)),
        scratch_shapes=[
            pltpu.VMEM((8, 128, 128), F32),
            pltpu.VMEM((13, 8, 24, 128), F32),
            pltpu.VMEM((2, 5, 8, 8, 128), I32),
            pltpu.VMEM((96, 8, 128), F32),
            pltpu.VMEM((CELLS, 128), F32),
        ],
        interpret=INTERPRET,
        compiler_params=pltpu.CompilerParams(vmem_limit_bytes=16 * 1024 * 1024),
    )(kept_near(message), kept_near(own), kept_near(strengths), kept_near(force), kept_near(half), kept_near(impact))


def steps(axis, by):
    count = lax.axis_size(axis)
    return [(i, i + by) for i in range(count) if 0 <= i + by < count]


def swaps(axis, start):
    count = lax.axis_size(axis)
    pairs = [(i, i + 1) for i in range(start, count - 1, 2)]
    return pairs + [(j, i) for i, j in pairs]


def local(displacement, velocity, acceleration, fibre_codes, contact_mask, bond_flags):
    adv, half, one, two, low, high = run_advance(displacement, velocity, acceleration, bond_flags)
    one = lax.ppermute(one, "ply", swaps("ply", 0))
    two = lax.ppermute(two, "ply", swaps("ply", 1))
    low = lax.ppermute(low, "stripe", steps("stripe", 1))
    high = lax.ppermute(high, "stripe", steps("stripe", -1))
    message = run_turn(one, two).reshape(TURNS, 1, WINDOW * 128)
    message = lax.all_to_all(message, "stripe", 0, 0)
    partial, own, strengths, rates, present, impact = run_pair(adv, fibre_codes, bond_flags, contact_mask)
    force = run_edge(low, high, own, rates, present, partial)
    message = message.reshape(TURNS * WINDOW, 128)
    new_velocity, new_acceleration = run_interface(message, own, strengths, force, half, impact)
    return adv, new_velocity, new_acceleration


def solution(mesh):
    state = P(None, "ply", None, "stripe", None)
    return jax.shard_map(
        local,
        mesh=mesh,
        in_specs=(state, state, state, P("ply", None), P("stripe", None), P("ply", None, "stripe", None)),
        out_specs=(state, state, state),
        check_vma=False,
    )
```
